512 devices in a mesh: row: 16 (over z), col: 32 (over x, y, core).
Axes of the slice: x: 4, y: 4, z: 16, core: 2. Of those that a mesh axis runs over, the one named last changes fastest.
Arguments:
- panel: float32 [4, 1536, 1, 32, 1536], P(None, 'row', None, 'col'), may hold values from -1 to 1, as said below
- inverse_blocks: float32 [4, 1536, 1536], P(None, 'row'), may hold values from -1 to 2, as said below
- right_side: float32 [48, 1, 32, 1536], P(None, None, 'col'), may hold values from -6 to 6
Outputs:
- solved: float32 [48, 4, 1536], P(None, None, 'row')
- updated: float32 [48, 1, 32, 1536], P(None, None, 'col', 'row')
The draws below stay inside these ranges and needn't reach their ends.
Inputs may be any that keep to these rules, and one draw needn't show every extreme that they name: panel is zero where the row index is below the column index as defined in its meaning (the factor is lower triangular). `inverse_blocks`: each inverse block is lower triangular with a positive diagonal.
All inputs are finite; a program needn't handle non-finite values.
Results may differ from the reference program's by a relative error of at most 0.0001.
Values sent between devices are 32-bit elements; how exact they have to be, the bound alone decides.
A program may use at most 64 MiB of HBM per device.

```python
import jax
import jax.numpy as jnp
from jax import lax

B = 1536
K = 4
RHS = 48
NJ = 1
NC = 32


def draw_panel(key, part):
    shape = (K, B, NJ, NC, B)
    values = jnp.clip(jax.random.normal(key, shape, jnp.float32), -4.0, 4.0)
    values = values * (K * B) ** (-0.5)
    kidx = jnp.arange(K).reshape(K, 1, 1, 1, 1)
    cidx = jnp.arange(B).reshape(1, B, 1, 1, 1)
    jidx = jnp.arange(NJ).reshape(1, 1, NJ, 1, 1)
    qidx = jnp.arange(NC).reshape(1, 1, 1, NC, 1)
    iidx = jnp.arange(B).reshape(1, 1, 1, 1, B)
    row_at = (jidx * NC + qidx) * B + iidx
    col_at = kidx * B + cidx
    return jnp.where(row_at >= col_at, values, 0.0).astype(jnp.float32)


def draw_inverse_blocks(key, part):
    first = jax.random.fold_in(key, 11)
    second = jax.random.fold_in(key, 23)
    shape = (K, B, B)
    lower = jnp.clip(jax.random.normal(first, shape, jnp.float32), -4.0, 4.0)
    lower = lower * 0.5 * B ** (-0.5)
    diag_vals = jax.random.uniform(second, (K, B, 1), jnp.float32, 0.5, 1.5)
    ridx = jnp.arange(B).reshape(1, B, 1)
    cidx = jnp.arange(B).reshape(1, 1, B)
    result = jnp.where(cidx < ridx, lower, 0.0) + jnp.where(cidx == ridx, diag_vals, 0.0)
    return result.astype(jnp.float32)


def level_of(rng, extent, cuts, least, top_value):
    gain = 1.0
    for axis_at, shards_of in cuts:
        steps = jax.random.uniform(jax.random.fold_in(jax.random.fold_in(rng, 6), axis_at), (shards_of,), jnp.float32, least / len(cuts), top_value / len(cuts))
        gain = gain * jnp.repeat(jnp.exp(steps), extent[axis_at] // shards_of).reshape((-1,) + (1,) * (len(extent) - 1 - axis_at))
    return gain


def normal_values(rng, extent, width, bound, split=(), held_as=jnp.bfloat16):
    entries = width * jax.random.normal(rng, extent, jnp.float32)
    if split:
        entries = entries * level_of(rng, extent, split, -0.22, 0.18)
    return jnp.clip(entries, -bound, bound).astype(held_as)


def setup_inputs(seed: int = 0) -> dict:
    keys = jax.random.split(jax.random.key(seed), 4)
    panel = draw_panel(jax.random.fold_in(keys[3], 71), 0)
    inverse_blocks = draw_inverse_blocks(jax.random.fold_in(keys[3], 71), 0)
    right_side = normal_values(keys[2], (RHS, NJ, NC, B), 1.0, 6.0, ((2, 32),), jnp.float32)
    return {"panel": panel, "inverse_blocks": inverse_blocks, "right_side": right_side}


def reference(panel, inverse_blocks, right_side):
    solved_list = []
    for step in range(K):
        jblock = step // NC
        qblock = step % NC
        total = jnp.zeros((RHS, B), jnp.float32)
        for prior in range(step):
            total = total + jnp.dot(solved_list[prior], panel[prior, :, jblock, qblock, :], precision=lax.Precision.HIGHEST, preferred_element_type=jnp.float32)
        residue = right_side[:, jblock, qblock, :] - total
        solved_list.append(jnp.dot(residue, inverse_blocks[step].T, precision=lax.Precision.HIGHEST, preferred_element_type=jnp.float32))
    stacked = jnp.stack(solved_list, axis=1)
    trailing = jnp.zeros((RHS, NJ, NC, B), jnp.float32)
    for step in range(K):
        trailing = trailing + jnp.einsum("rc,cjqi->rjqi", stacked[:, step, :], panel[step], precision=lax.Precision.HIGHEST)
    return stacked, right_side - trailing
```

```python
import jax
import jax.numpy as jnp
from jax import lax
from jax.experimental import pallas as pl
from jax.experimental.pallas import tpu as pltpu
from jax.sharding import PartitionSpec as P

MESH = pl.DeviceIdType.MESH
F32 = jnp.float32
HI = lax.Precision.HIGHEST
ROWS, COLS = 16, 32
STEPS, RHS, BLK, SLC = 4, 48, 1536, 96
TILES = BLK // 128
CHAIN = (4, 6, 8, 10, 24, 26)
PART = RHS // len(CHAIN)
CUT = BLK // 4


def dot(left, right):
    return lax.dot_general(left, right, (((1,), (0,)), ((), ())), precision=HI, preferred_element_type=F32)


def dot_t(left, right):
    return lax.dot_general(left, right, (((1,), (1,)), ((), ())), precision=HI, preferred_element_type=F32)


def kernel(
    panel_ref,
    inverse_ref,
    right_ref,
    solved_ref,
    updated_ref,
    flat,
    cut,
    rep_flat,
    inv,
    right_flat,
    right,
    pieces,
    base,
    base_in,
    rs_out,
    rs_in,
    residue,
    mine,
    acc,
    packed,
    fin_in,
    load_sem,
    rep_send,
    rep_recv,
    piece_send,
    piece_recv,
    base_send,
    base_recv,
    rs_send,
    rs_recv,
    ag_send,
    ag_recv,
    fin_send,
    fin_recv,
):
    p = lax.axis_index("row")
    q = lax.axis_index("col")
    is_chain = q == CHAIN[0]
    g = jnp.int32(0)
    for n, c in enumerate(CHAIN):
        is_chain = is_chain | (q == c)
        g = g + jnp.where(q == c, n, 0)

    def wait(ref, sem):
        pltpu.make_async_copy(ref, ref, sem).wait()

    def push(src, dst, send, recv, where):
        pltpu.make_async_remote_copy(
            src_ref=src, dst_ref=dst, send_sem=send, recv_sem=recv, device_id=where, device_id_type=MESH
        ).start()

    load_right = pltpu.make_async_copy(right_ref, right_flat, load_sem.at[0])
    load_panel = pltpu.make_async_copy(panel_ref, flat, load_sem.at[1])
    load_inv = pltpu.make_async_copy(inverse_ref, inv, load_sem.at[2])
    load_right.start()
    load_inv.start()
    load_panel.start()

    barrier = pltpu.get_barrier_semaphore()

    def hello_plane(i, _):
        pl.semaphore_signal(barrier, inc=1, device_id=(p, lax.rem(q + i, COLS)), device_id_type=MESH)
        return 0

    def hello_ring(i, _):
        pl.semaphore_signal(barrier, inc=1, device_id=(lax.rem(p + i, ROWS), q), device_id_type=MESH)
        return 0

    lax.fori_loop(1, ROWS, hello_ring, 0)
    lax.fori_loop(1, COLS, hello_plane, 0)

    load_right.wait()
    for j in range(TILES):
        right[:, 128 * j : 128 * (j + 1)] = right_flat[pl.ds(j, RHS, stride=TILES), :]
    load_inv.wait()

    @pl.when(q == 0)
    def _():
        first = dot_t(right[...], inv[0])
        pieces[0, :, 0:SLC] = first

    pl.semaphore_wait(barrier, ROWS - 1 + COLS - 1)
    load_panel.wait()

    def spread_first(i, _):
        push(pieces.at[0], pieces.at[0], piece_send.at[0], piece_recv.at[0], (p, lax.rem(q + i, COLS)))
        return 0

    @pl.when(q == 0)
    def _():
        lax.fori_loop(1, COLS, spread_first, 0)

    for k in (2, 3):

        @pl.when(q == k)
        def _():
            for n, c in enumerate(CHAIN):
                push(
                    flat.at[pl.ds((k - 1) * SLC * TILES, SLC * TILES)],
                    rep_flat.at[k - 2],
                    rep_send.at[n],
                    rep_recv.at[k - 2],
                    (p, c),
                )

    def panel_block(k):
        return [flat[pl.ds(k * SLC * TILES + j, SLC, stride=TILES), :] for j in range(TILES)]

    def send_base(k):
        for n, c in enumerate(CHAIN):
            push(
                base.at[pl.ds(PART * n, PART)],
                base_in.at[k - 1],
                base_send.at[0],
                base_recv.at[k - 1],
                (p, c),
            )

    own = jnp.where(p == 0, 1.0, 0.0).astype(F32)

    @pl.when(q == 1)
    def _():
        wait(pieces.at[0], piece_recv.at[0])
        for j, block in enumerate(panel_block(0)):
            at = slice(128 * j, 128 * (j + 1))
            base[:, at] = own * right[:, at] - dot(pieces[0, :, 0:SLC], block)
        send_base(1)

    lane = lax.broadcasted_iota(jnp.int32, (SLC, 128), 1)

    def cut_block(k, _):
        for n in range(ROWS):
            tile, shift = (SLC * n) // 128, (SLC * n) % 128
            block = flat[pl.ds(k * SLC * TILES + tile, SLC, stride=TILES), :]
            if shift:
                block = pltpu.roll(block, 128 - shift, 1)
                if shift > 128 - SLC:
                    after = flat[pl.ds(k * SLC * TILES + tile + 1, SLC, stride=TILES), :]
                    block = jnp.where(lane < 128 - shift, block, pltpu.roll(after, 128 - shift, 1))
            cut[k, :, 128 * n : 128 * (n + 1)] = block
        return 0

    lax.fori_loop(0, STEPS, cut_block, 0)

    def add_piece(k):
        piece = pieces[k, :, 0:SLC]
        for n in range(0, ROWS, 2):
            term = dot(piece, cut[k, :, 128 * n : 128 * (n + 2)])
            for h in range(2):
                value = term[:, 128 * h : 128 * (h + 1)]
                if k == 0:
                    acc[n + h] = value
                else:
                    acc[n + h] += value

    @pl.when(q == 2)
    def _():
        wait(pieces.at[0], piece_recv.at[0])
        for j, block in enumerate(panel_block(0)):
            at = slice(128 * j, 128 * (j + 1))
            base[:, at] = own * right[:, at] - dot(pieces[0, :, 0:SLC], block)
        send_base(2)

    @pl.when(q == 3)
    def _():
        wait(pieces.at[0], piece_recv.at[0])
        wait(pieces.at[1], piece_recv.at[1])
        first, second = panel_block(0), panel_block(1)
        for j in range(TILES):
            at = slice(128 * j, 128 * (j + 1))
            term = dot(pieces[0, :, 0:SLC], first[j]) + dot(pieces[1, :, 0:SLC], second[j])
            base[:, at] = own * right[:, at] - term
        send_base(3)

    def far_first(i):
        return lax.rem(p + 8 + (1 - 2 * lax.rem(i, 2)) * lax.div(i + 1, 2), ROWS)

    @pl.when(is_chain)
    def _():
        rows = pl.ds(pl.multiple_of(PART * g, PART), PART)
        my_cut = pl.ds(pl.multiple_of(CUT * lax.rem(p, 4), 128), CUT)

        def spread(k):
            def send(i, _):
                push(
                    mine.at[k],
                    pieces.at[k, rows],
                    piece_send.at[k],
                    piece_recv.at[k],
                    (p, lax.rem(q + i, COLS)),
                )
                return 0

            lax.fori_loop(1, COLS, send, 0)

        for k in range(1, STEPS):
            wait(base_in.at[k - 1], base_recv.at[k - 1])
            if k == 1:
                rs_out[0] = base_in[0]
            else:
                wait(rep_flat.at[k - 2], rep_recv.at[k - 2])
                for j in range(TILES):
                    at = slice(128 * j, 128 * (j + 1))
                    block = rep_flat[k - 2, pl.ds(j, SLC, stride=TILES), :]
                    rs_out[k - 1, :, at] = base_in[k - 1, :, at] - dot(mine[k - 1, :, 0:SLC], block)

            def scatter(i, _):
                to = far_first(i)
                part = pl.ds(pl.multiple_of(CUT * lax.rem(to, 4), 128), CUT)
                slot = lax.rem(p - to + ROWS, ROWS) - 1
                push(
                    rs_out.at[k - 1, :, part],
                    rs_in.at[k - 1, slot],
                    rs_send.at[k - 1],
                    rs_recv.at[k - 1],
                    (to, q),
                )
                return 0

            lax.fori_loop(0, ROWS - 1, scatter, 0)
            if k == 1:
                wait(pieces.at[0], piece_recv.at[0])
            else:
                spread(k - 1)
                wait(pieces.at[k - 1, pl.ds(0, RHS - PART)], piece_recv.at[k - 1])
                pieces[k - 1, rows, :] = mine[k - 1]
            add_piece(k - 1)

            wait(rs_in.at[k - 1], rs_recv.at[k - 1])
            total = rs_out[k - 1, :, my_cut]
            for n in range(ROWS - 1):
                total = total + rs_in[k - 1, n]
            residue[k - 1, :, my_cut] = total
            for d in (2, -1, 1):
                push(
                    residue.at[k - 1, :, my_cut],
                    residue.at[k - 1, :, my_cut],
                    ag_send.at[k - 1],
                    ag_recv.at[k - 1],
                    (lax.rem(p - d + ROWS, ROWS), q),
                )
            wait(residue.at[k - 1, :, pl.ds(0, 3 * CUT)], ag_recv.at[k - 1])
            mine[k, :, 0:SLC] = dot_t(residue[k - 1], inv[k])
            mine[k, :, SLC:] = jnp.zeros((PART, 128 - SLC), F32)

        spread(STEPS - 1)
        last = STEPS - 1
        wait(pieces.at[last, pl.ds(0, RHS - PART)], piece_recv.at[last])
        pieces[last, rows, :] = mine[last]

    @pl.when(jnp.logical_not(is_chain))
    def _():
        @pl.when(q > 3)
        def _():
            wait(pieces.at[0], piece_recv.at[0])

        add_piece(0)

        @pl.when(q != 3)
        def _():
            wait(pieces.at[1], piece_recv.at[1])

        add_piece(1)
        wait(pieces.at[2], piece_recv.at[2])
        add_piece(2)
        wait(pieces.at[3], piece_recv.at[3])

    add_piece(STEPS - 1)

    wide = lax.broadcasted_iota(jnp.int32, (8, 128), 1)
    for n in range(ROWS):
        rest = acc[n, RHS - 8 : RHS, :]
        for a in range(3):
            beside = pltpu.roll(rest, SLC - 32 * a, 1)
            packed[n, 8 * a : 8 * (a + 1), :] = jnp.where(wide < SLC, acc[n, 8 * a : 8 * (a + 1), :], beside)
        packed[n, 24 : RHS - 8, :] = acc[n, 24 : RHS - 8, :]

    def finish(i, _):
        to = far_first(i)
        slot = lax.rem(p - to + ROWS, ROWS) - 1
        push(
            packed.at[to],
            fin_in.at[slot],
            fin_send,
            fin_recv,
            (to, q),
        )
        return 0

    lax.fori_loop(0, ROWS - 1, finish, 0)
    for k in range(STEPS):
        solved_ref[:, k, :] = pieces[k, :, 0:SLC]

    tile = lax.div(3 * p, 4)
    shift = 32 * lax.rem(3 * p, 4)
    here = right[:, pl.ds(pl.multiple_of(128 * tile, 128), 128)]
    after = right[:, pl.ds(pl.multiple_of(128 * jnp.minimum(tile + 1, TILES - 1), 128), 128)]
    turn = lax.rem(128 - shift, 128)
    lanes = lax.broadcasted_iota(jnp.int32, (RHS, 128), 1)
    total = jnp.where(lanes < 128 - shift, pltpu.roll(here, turn, 1), pltpu.roll(after, turn, 1))
    term = packed[p]
    wait(fin_in, fin_recv)
    for n in range(ROWS - 1):
        term = term + fin_in[n]
    updated_ref[0 : RHS - 8, :] = (total[0 : RHS - 8, :] - term)[:, 0:SLC]
    last = jnp.where(wide < 32, pltpu.roll(term[0:8, :], 32, 1), pltpu.roll(term[8:16, :], 64, 1))
    last = jnp.where(wide < 64, last, pltpu.roll(term[16:24, :], SLC, 1))
    updated_ref[RHS - 8 : RHS, :] = (total[RHS - 8 : RHS, :] - last)[:, 0:SLC]

    wait(fin_in, fin_send)

    @pl.when(q == 0)
    def _():
        wait(flat.at[pl.ds(0, (COLS - 1) * RHS)], piece_send.at[0])

    @pl.when((q == 2) | (q == 3))
    def _():
        for n in range(len(CHAIN)):
            wait(rep_flat.at[0], rep_send.at[n])

    @pl.when((q >= 1) & (q <= 3))
    def _():
        wait(base, base_send.at[0])

    @pl.when(is_chain)
    def _():
        for k in range(1, STEPS):
            wait(rs_in.at[k - 1], rs_send.at[k - 1])
            wait(residue.at[k - 1, :, pl.ds(0, 3 * CUT)], ag_send.at[k - 1])
            wait(flat.at[pl.ds(0, (COLS - 1) * PART)], piece_send.at[k])


def body(panel, inverse_blocks, right_side):
    hbm = pl.BlockSpec(memory_space=pl.ANY)
    vmem = pl.BlockSpec(memory_space=pltpu.VMEM)
    dma = pltpu.SemaphoreType.DMA
    solved, updated = pl.pallas_call(
        kernel,
        out_shape=(
            jax.ShapeDtypeStruct((RHS, STEPS, SLC), F32),
            jax.ShapeDtypeStruct((RHS, SLC), F32),
        ),
        in_specs=[hbm, hbm, hbm],
        out_specs=(vmem, vmem),
        scratch_shapes=[
            pltpu.VMEM((STEPS * SLC * TILES, 128), F32),
            pltpu.VMEM((STEPS, SLC, ROWS * 128), F32),
            pltpu.VMEM((2, SLC * TILES, 128), F32),
            pltpu.VMEM((STEPS, SLC, BLK), F32),
            pltpu.VMEM((RHS * TILES, 128), F32),
            pltpu.VMEM((RHS, BLK), F32),
            pltpu.VMEM((STEPS, RHS, 128), F32),
            pltpu.VMEM((RHS, BLK), F32),
            pltpu.VMEM((3, PART, BLK), F32),
            pltpu.VMEM((3, PART, BLK), F32),
            pltpu.VMEM((3, ROWS - 1, PART, CUT), F32),
            pltpu.VMEM((3, PART, BLK), F32),
            pltpu.VMEM((STEPS, PART, 128), F32),
            pltpu.VMEM((ROWS, RHS, 128), F32),
            pltpu.VMEM((ROWS, RHS - 8, 128), F32),
            pltpu.VMEM((ROWS - 1, RHS - 8, 128), F32),
            dma((3,)),
            dma((len(CHAIN),)),
            dma((2,)),
            dma((STEPS,)),
            dma((STEPS,)),
            dma((1,)),
            dma((3,)),
            dma((3,)),
            dma((3,)),
            dma((3,)),
            dma((3,)),
            dma,
            dma,
        ],
        compiler_params=pltpu.CompilerParams(
            collective_id=0, has_side_effects=True
        ),
        name="solve",
    )(
        panel.reshape(STEPS * SLC * TILES, 128),
        inverse_blocks,
        right_side.reshape(RHS * TILES, 128),
    )
    return solved, updated.reshape(RHS, 1, 1, SLC)


def solution(mesh):
    placed = (P(None, "row", None, "col", None), P(None, "row", None), P(None, None, "col", None))
    return jax.shard_map(
        body,
        mesh=mesh,
        in_specs=placed,
        out_specs=(P(None, None, "row"), P(None, None, "col", "row")),
        check_vma=False,
    )
```

```python
import jax
import jax.numpy as jnp
from jax import lax
from jax.experimental import pallas as pl
from jax.experimental.pallas import tpu as pltpu
from jax.sharding import PartitionSpec as P

MESH = pl.DeviceIdType.MESH
F32 = jnp.float32
BF16 = jnp.bfloat16
ROWS, COLS = 16, 32
STEPS, RHS, BLK, SLC = 4, 48, 1536, 96
TILES = BLK // 128
CHAIN = (4, 6, 8, 10, 24, 26)
PART = RHS // len(CHAIN)
CUT = BLK // 4
ORDER = (2, 4, 6, 8, 14, 12, 10, 1, 3, 5, 7, 15, 13, 11, 9, 0)


def split(value):
    high = value.astype(BF16)
    return high, (value - high.astype(F32)).astype(BF16)


def dot3(left, right, axis):
    rows = left.shape[0]
    high, low = split(left)
    dims = (((1,), (axis,)), ((), ()))
    both = lax.dot_general(jnp.concatenate([high, low], 0), right[0], dims, preferred_element_type=F32)
    rest = lax.dot_general(high, right[1], dims, preferred_element_type=F32)
    return both[:rows] + (both[rows:] + rest)


def kernel(
    panel_ref,
    inverse_ref,
    right_ref,
    solved_ref,
    updated_ref,
    flat,
    cut_high,
    cut_low,
    rep_flat,
    block_high,
    block_low,
    inv,
    inv_high,
    inv_low,
    right_flat,
    right,
    pieces,
    base,
    base_in,
    rs_out,
    rs_in,
    residue,
    mine,
    acc,
    packed,
    near_in,
    far_in,
    panel_sem,
    inverse_sem,
    right_sem,
    rep_send,
    rep_recv,
    rep_turn,
    first_send,
    piece_send,
    piece_recv,
    base_send,
    base_recv,
    rs_send,
    rs_recv,
    ag_send,
    ag_recv,
    near_send,
    near_recv,
    far_send,
    far_recv,
):
    p = lax.axis_index("row")
    q = lax.axis_index("col")
    is_chain = q == CHAIN[0]
    g = jnp.int32(0)
    for n, c in enumerate(CHAIN):
        is_chain = is_chain | (q == c)
        g = g + jnp.where(q == c, n, 0)

    def wait(ref, sem):
        pltpu.make_async_copy(ref, ref, sem).wait()

    def push(src, dst, send, recv, where):
        pltpu.make_async_remote_copy(
            src_ref=src, dst_ref=dst, send_sem=send, recv_sem=recv, device_id=where, device_id_type=MESH
        ).start()

    def load_inverse(k):
        return pltpu.make_async_copy(inverse_ref.at[k], inv.at[k], inverse_sem.at[k])

    def load_panel(k):
        part = pl.ds(k * SLC * TILES, SLC * TILES)
        return pltpu.make_async_copy(panel_ref.at[part], flat.at[part], panel_sem.at[k])

    load_right = pltpu.make_async_copy(right_ref, right_flat, right_sem)
    load_right.start()

    @pl.when(q == 0)
    def _():
        load_inverse(0).start()

    for k in range(STEPS):
        load_panel(k).start()

    barrier = pltpu.get_barrier_semaphore()

    def hello(row, col):
        pl.semaphore_signal(barrier, inc=1, device_id=(row, col), device_id_type=MESH)

    @pl.when(q == 1)
    def _():
        hello(p, 0)

    @pl.when(is_chain | (q == 3))
    def _():
        hello(p, 1)
        hello(p, 2)

    for c in CHAIN:

        @pl.when(q != c)
        def _():
            hello(p, c)

    @pl.when((q == 2) | (q > 3))
    def _():
        hello(p, 3)

    @pl.when(q > 3)
    def _():
        def ring(i, _):
            hello(lax.rem(p + i, ROWS), q)
            return 0

        lax.fori_loop(1, ROWS, ring, 0)

    @pl.when(is_chain)
    def _():
        for k in range(1, STEPS):
            load_inverse(k).start()

    load_right.wait()
    for j in range(TILES):
        right[:, 128 * j : 128 * (j + 1)] = right_flat[pl.ds(j, RHS, stride=TILES), :]

    def panel_tile(k, j):
        return flat[pl.ds(k * SLC * TILES + j, SLC, stride=TILES), :]

    def split_block(n, tile):
        for j in range(TILES):
            at = slice(128 * j, 128 * (j + 1))
            block_high[n, :, at], block_low[n, :, at] = split(tile(j))

    own = jnp.where(p == 0, 1.0, 0.0).astype(F32)

    def send_base(k):
        for n, c in enumerate(CHAIN):
            push(
                base.at[pl.ds(PART * n, PART)],
                base_in.at[k - 1],
                base_send,
                base_recv.at[k - 1],
                (p, c),
            )

    def block(n):
        return block_high[n], block_low[n]

    @pl.when(q == 0)
    def _():
        load_inverse(0).wait()
        pieces[0, :, 0:SLC] = dot3(right[...], split(inv[0]), 1)
        pl.semaphore_wait(barrier, 1)
        push(pieces.at[0], pieces.at[0], first_send, piece_recv.at[0], (p, 1))

    @pl.when(q == 1)
    def _():
        load_panel(0).wait()
        split_block(0, lambda j: panel_tile(0, j))
        pl.semaphore_wait(barrier, len(CHAIN) + 1)
        wait(pieces.at[0], piece_recv.at[0])
        base[...] = own * right[...] - dot3(pieces[0, :, 0:SLC], block(0), 0)
        send_base(1)
        push(pieces.at[0], pieces.at[0], first_send, piece_recv.at[0], (p, 3))

    def send_block(k):
        for n, c in enumerate(CHAIN):
            push(
                flat.at[pl.ds((k - 1) * SLC * TILES, SLC * TILES)],
                rep_flat.at[k - 2],
                rep_send.at[n],
                rep_recv.at[k - 2],
                (p, c),
            )

    @pl.when(q == 2)
    def _():
        load_panel(1).wait()
        pl.semaphore_wait(barrier, len(CHAIN) + 1)
        send_block(2)
        load_panel(0).wait()
        split_block(0, lambda j: panel_tile(0, j))
        wait(pieces.at[0], piece_recv.at[0])
        base[...] = own * right[...] - dot3(pieces[0, :, 0:SLC], block(0), 0)
        send_base(2)
        for n in range(len(CHAIN)):
            wait(rep_flat.at[0], rep_send.at[n])
        pl.semaphore_signal(rep_turn, inc=1, device_id=(p, 3), device_id_type=MESH)

    @pl.when(q == 3)
    def _():
        for k in range(2):
            load_panel(k).wait()
            split_block(k, lambda j: panel_tile(k, j))
        load_panel(2).wait()
        pl.semaphore_wait(barrier, COLS - 3)
        wait(pieces.at[0], piece_recv.at[0])
        push(pieces.at[0], pieces.at[0], first_send, piece_recv.at[0], (p, 2))

        def spread_first(i, _):
            push(pieces.at[0], pieces.at[0], piece_send.at[0], piece_recv.at[0], (p, i))
            return 0

        lax.fori_loop(4, COLS, spread_first, 0)
        base[...] = own * right[...] - dot3(pieces[0, :, 0:SLC], block(0), 0)
        pl.semaphore_wait(rep_turn, 1)
        send_block(3)

    @pl.when(is_chain)
    def _():
        pl.semaphore_wait(barrier, ROWS - 1 + COLS - 1)

    @pl.when((q > 3) & jnp.logical_not(is_chain))
    def _():
        pl.semaphore_wait(barrier, ROWS - 1)

    lane = lax.broadcasted_iota(jnp.int32, (SLC, 128), 1)

    def cut_block(k, _):
        for n in range(ROWS):
            tile, shift = (SLC * n) // 128, (SLC * n) % 128
            value = panel_tile(k, tile)
            if shift:
                value = pltpu.roll(value, 128 - shift, 1)
                if shift > 128 - SLC:
                    after = pltpu.roll(panel_tile(k, tile + 1), 128 - shift, 1)
                    value = jnp.where(lane < 128 - shift, value, after)
            at = slice(128 * n, 128 * (n + 1))
            cut_high[k, :, at], cut_low[k, :, at] = split(value)
        return 0

    for k in range(STEPS):
        ready = {0: (1, 2, 3), 1: (2, 3), 2: (3,), 3: ()}[k]
        pending = q >= 0
        for c in ready:
            pending = pending & (q != c)

        @pl.when(pending)
        def _():
            load_panel(k).wait()

    lax.fori_loop(0, STEPS, cut_block, 0)

    def add_piece(k):
        piece = pieces[k, :, 0:SLC]
        for n in range(0, ROWS, 2):
            at = slice(128 * n, 128 * (n + 2))
            term = dot3(piece, (cut_high[k, :, at], cut_low[k, :, at]), 0)
            for h in range(2):
                value = term[:, 128 * h : 128 * (h + 1)]
                if k == 0:
                    acc[n + h] = value
                else:
                    acc[n + h] += value

    def far_first(i):
        return lax.rem(p + 8 + (1 - 2 * lax.rem(i, 2)) * lax.div(i + 1, 2), ROWS)

    @pl.when(is_chain)
    def _():
        rows = pl.ds(pl.multiple_of(PART * g, PART), PART)
        my_cut = pl.ds(pl.multiple_of(CUT * lax.rem(p, 4), 128), CUT)

        def spread(k):
            def send(i, _):
                push(
                    mine.at[k],
                    pieces.at[k, rows],
                    piece_send.at[k],
                    piece_recv.at[k],
                    (p, lax.rem(q + i, COLS)),
                )
                return 0

            lax.fori_loop(1, COLS, send, 0)

        for k in range(1, STEPS):
            load_inverse(k).wait()
            inv_high[k], inv_low[k] = split(inv[k])

        for k in range(1, STEPS):
            wait(base_in.at[k - 1], base_recv.at[k - 1])
            if k == 1:
                rs_out[0] = base_in[0]
            else:
                rs_out[k - 1] = base_in[k - 1] - dot3(mine[k - 1, :, 0:SLC], block(k - 2), 0)

            def scatter(i, _):
                to = far_first(i)
                part = pl.ds(pl.multiple_of(CUT * lax.rem(to, 4), 128), CUT)
                slot = lax.rem(p - to + ROWS, ROWS) - 1
                push(
                    rs_out.at[k - 1, :, part],
                    rs_in.at[k - 1, slot],
                    rs_send.at[k - 1],
                    rs_recv.at[k - 1],
                    (to, q),
                )
                return 0

            lax.fori_loop(0, ROWS - 1, scatter, 0)
            if k == 1:
                wait(pieces.at[0], piece_recv.at[0])
            else:
                spread(k - 1)
                wait(pieces.at[k - 1, pl.ds(0, RHS - PART)], piece_recv.at[k - 1])
                pieces[k - 1, rows, :] = mine[k - 1]
            add_piece(k - 1)

            wait(rs_in.at[k - 1], rs_recv.at[k - 1])
            total = rs_out[k - 1, :, my_cut]
            for n in range(ROWS - 1):
                total = total + rs_in[k - 1, n]
            residue[k - 1, :, my_cut] = total
            for d in (2, -1, 1):
                push(
                    residue.at[k - 1, :, my_cut],
                    residue.at[k - 1, :, my_cut],
                    ag_send.at[k - 1],
                    ag_recv.at[k - 1],
                    (lax.rem(p - d + ROWS, ROWS), q),
                )
            if k < STEPS - 1:
                wait(rep_flat.at[k - 1], rep_recv.at[k - 1])
                split_block(k - 1, lambda j: rep_flat[k - 1, pl.ds(j, SLC, stride=TILES), :])
            wait(residue.at[k - 1, :, pl.ds(0, 3 * CUT)], ag_recv.at[k - 1])
            mine[k, :, 0:SLC] = dot3(residue[k - 1], (inv_high[k], inv_low[k]), 1)
            mine[k, :, SLC:] = jnp.zeros((PART, 128 - SLC), F32)

        last = STEPS - 1
        spread(last)
        wait(pieces.at[last, pl.ds(0, RHS - PART)], piece_recv.at[last])
        pieces[last, rows, :] = mine[last]

    @pl.when(jnp.logical_not(is_chain))
    def _():
        @pl.when(q > 3)
        def _():
            wait(pieces.at[0], piece_recv.at[0])

        add_piece(0)
        wait(pieces.at[1], piece_recv.at[1])

        @pl.when(q == 3)
        def _():
            base[...] = base[...] - dot3(pieces[1, :, 0:SLC], block(1), 0)
            send_base(3)

        add_piece(1)
        wait(pieces.at[2], piece_recv.at[2])
        add_piece(2)
        wait(pieces.at[3], piece_recv.at[3])

    add_piece(STEPS - 1)

    wide = lax.broadcasted_iota(jnp.int32, (8, 128), 1)
    for slot, d in enumerate(ORDER):
        n = lax.rem(p + d, ROWS)
        rest = acc[n, RHS - 8 : RHS, :]
        for a in range(3):
            beside = pltpu.roll(rest, SLC - 32 * a, 1)
            packed[slot, 8 * a : 8 * (a + 1), :] = jnp.where(wide < SLC, acc[n, 8 * a : 8 * (a + 1), :], beside)
        packed[slot, 24 : RHS - 8, :] = acc[n, 24 : RHS - 8, :]
        if slot in (3, 6):
            part = pl.ds(0, 4) if slot == 3 else pl.ds(4, 3)
            to = 1 if slot == 3 else ROWS - 1
            push(packed.at[part], near_in.at[part], near_send, near_recv, (lax.rem(p + to, ROWS), q))

    def finish(slot):
        push(
            packed.at[slot],
            far_in.at[slot - 7],
            far_send,
            far_recv,
            (lax.rem(p + ORDER[slot], ROWS), q),
        )

    finish(14)
    solved_ref[...] = pieces[:, :, 0:SLC]

    tile = lax.div(3 * p, 4)
    shift = 32 * lax.rem(3 * p, 4)
    here = right[:, pl.ds(pl.multiple_of(128 * tile, 128), 128)]
    after = right[:, pl.ds(pl.multiple_of(128 * jnp.minimum(tile + 1, TILES - 1), 128), 128)]
    turn = lax.rem(128 - shift, 128)
    lanes = lax.broadcasted_iota(jnp.int32, (RHS, 128), 1)
    total = jnp.where(lanes < 128 - shift, pltpu.roll(here, turn, 1), pltpu.roll(after, turn, 1))

    wait(near_in, near_recv)
    for slot in (10, 9, 13, 8, 12, 7, 11):
        packed[slot] = packed[slot] + near_in[slot - 7]
        finish(slot)
    term = packed[15]
    wait(far_in, far_recv)
    for n in range(8):
        term = term + far_in[n]
    updated_ref[0 : RHS - 8, :] = (total[0 : RHS - 8, :] - term)[:, 0:SLC]
    last = jnp.where(wide < 32, pltpu.roll(term[0:8, :], 32, 1), pltpu.roll(term[8:16, :], 64, 1))
    last = jnp.where(wide < 64, last, pltpu.roll(term[16:24, :], SLC, 1))
    updated_ref[RHS - 8 : RHS, :] = (total[RHS - 8 : RHS, :] - last)[:, 0:SLC]

    wait(near_in, near_send)
    wait(far_in, far_send)

    @pl.when((q == 0) | (q == 1) | (q == 3))
    def _():
        wait(pieces.at[0], first_send)

    @pl.when((q >= 1) & (q <= 3))
    def _():
        wait(base, base_send)

    @pl.when(q == 3)
    def _():
        wait(flat.at[pl.ds(0, (COLS - 4) * RHS)], piece_send.at[0])
        for n in range(len(CHAIN)):
            wait(rep_flat.at[0], rep_send.at[n])

    @pl.when(is_chain)
    def _():
        for k in range(1, STEPS):
            wait(rs_in.at[k - 1], rs_send.at[k - 1])
            wait(residue.at[k - 1, :, pl.ds(0, 3 * CUT)], ag_send.at[k - 1])
            wait(flat.at[pl.ds(0, (COLS - 1) * PART)], piece_send.at[k])


def body(panel, inverse_blocks, right_side):
    hbm = pl.BlockSpec(memory_space=pl.ANY)
    vmem = pl.BlockSpec(memory_space=pltpu.VMEM)
    dma = pltpu.SemaphoreType.DMA
    solved, updated = pl.pallas_call(
        kernel,
        out_shape=(
            jax.ShapeDtypeStruct((STEPS, RHS, SLC), F32),
            jax.ShapeDtypeStruct((RHS, SLC), F32),
        ),
        in_specs=[hbm, hbm, hbm],
        out_specs=(vmem, vmem),
        scratch_shapes=[
            pltpu.VMEM((STEPS * SLC * TILES, 128), F32),
            pltpu.VMEM((STEPS, SLC, ROWS * 128), BF16),
            pltpu.VMEM((STEPS, SLC, ROWS * 128), BF16),
            pltpu.VMEM((2, SLC * TILES, 128), F32),
            pltpu.VMEM((2, SLC, BLK), BF16),
            pltpu.VMEM((2, SLC, BLK), BF16),
            pltpu.VMEM((STEPS, SLC, BLK), F32),
            pltpu.VMEM((STEPS, SLC, BLK), BF16),
            pltpu.VMEM((STEPS, SLC, BLK), BF16),
            pltpu.VMEM((RHS * TILES, 128), F32),
            pltpu.VMEM((RHS, BLK), F32),
            pltpu.VMEM((STEPS, RHS, 128), F32),
            pltpu.VMEM((RHS, BLK), F32),
            pltpu.VMEM((3, PART, BLK), F32),
            pltpu.VMEM((3, PART, BLK), F32),
            pltpu.VMEM((3, ROWS - 1, PART, CUT), F32),
            pltpu.VMEM((3, PART, BLK), F32),
            pltpu.VMEM((STEPS, PART, 128), F32),
            pltpu.VMEM((ROWS, RHS, 128), F32),
            pltpu.VMEM((ROWS, RHS - 8, 128), F32),
            pltpu.VMEM((7, RHS - 8, 128), F32),
            pltpu.VMEM((8, RHS - 8, 128), F32),
            dma((STEPS,)),
            dma((STEPS,)),
            dma,
            dma((len(CHAIN),)),
            dma((2,)),
            pltpu.SemaphoreType.REGULAR,
            dma,
            dma((STEPS,)),
            dma((STEPS,)),
            dma,
            dma((3,)),
            dma((3,)),
            dma((3,)),
            dma((3,)),
            dma((3,)),
            dma,
            dma,
            dma,
            dma,
        ],
        compiler_params=pltpu.CompilerParams(collective_id=0, has_side_effects=True),
        name="solve",
    )(
        panel.reshape(STEPS * SLC * TILES, 128),
        inverse_blocks,
        right_side.reshape(RHS * TILES, 128),
    )
    return jnp.transpose(solved, (1, 0, 2)), updated.reshape(RHS, 1, 1, SLC)


def solution(mesh):
    placed = (P(None, "row", None, "col", None), P(None, "row", None), P(None, None, "col", None))
    return jax.shard_map(
        body,
        mesh=mesh,
        in_specs=placed,
        out_specs=(P(None, None, "row"), P(None, None, "col", "row")),
        check_vma=False,
    )
```

```python
import jax
import jax.numpy as jnp
from jax import lax
from jax.experimental import pallas as pl
from jax.experimental.pallas import tpu as pltpu
from jax.sharding import PartitionSpec as P

MESH = pl.DeviceIdType.MESH
F32 = jnp.float32
BF16 = jnp.bfloat16
ROWS, COLS = 16, 32
STEPS, RHS, BLK, SLC = 4, 48, 1536, 96
TILES = BLK // 128
CHAIN = (4, 6, 8, 10, 12, 14, 16, 18, 24, 26, 28, 30)
RELAYS = {5: (4, 6, 14, 30), 11: (10, 8, 12, 18), 27: (26, 24, 28, 16)}
THIRD = SLC * BLK // 128 // 3
PART = RHS // len(CHAIN)
CUT = BLK // 4
ORDER = (2, 4, 6, 8, 14, 12, 10, 1, 3, 5, 7, 15, 13, 11, 9, 0)
AROUND = sorted(
    [(x, y, c) for x in range(4) for y in range(4) for c in range(2) if x or y or c],
    key=lambda d: (-min(d[0], 4 - d[0]) - min(d[1], 4 - d[1]), d),
)
TAIL = RHS - RHS // 4


def split(value):
    high = value.astype(BF16)
    return high, (value - high.astype(F32)).astype(BF16)


def dot3(left, right, axis):
    rows = left.shape[0]
    high = left.astype(BF16)
    wide = high.astype(F32)
    stacked = jnp.concatenate([wide, left - wide], 0).astype(BF16)
    dims = (((1,), (axis,)), ((), ()))
    both = lax.dot_general(stacked, right[0], dims, preferred_element_type=F32)
    rest = lax.dot_general(high, right[1], dims, preferred_element_type=F32)
    return both[:rows] + (both[rows:] + rest)


def kernel(
    panel_ref,
    inverse_ref,
    right_ref,
    solved_ref,
    updated_ref,
    flat,
    cut_high,
    cut_low,
    rep_flat,
    block_high,
    block_low,
    inv,
    inv_high,
    inv_low,
    right_flat,
    right,
    pieces,
    parts,
    base,
    base_out,
    base_in,
    rs_out,
    rs_in,
    residue,
    mine,
    acc,
    packed,
    near_in,
    far_in,
    panel_sem,
    inverse_sem,
    right_sem,
    rep_send,
    rep_recv,
    rep_turn,
    relay_send,
    first_send,
    piece_send,
    piece_recv,
    base_send,
    base_recv,
    rs_send,
    rs_recv,
    ag_send,
    ag_recv,
    near_send,
    near_recv,
    far_send,
    far_recv,
):
    p = lax.axis_index("row")
    q = lax.axis_index("col")
    is_chain = (lax.rem(q, 2) == 0) & (q > 3) & (q != 20) & (q != 22)
    g = jnp.where(q < 20, lax.div(q - 4, 2), lax.div(q - 8, 2))
    is_relay = (q == 5) | (q == 11) | (q == 27)

    def wait(ref, sem):
        pltpu.make_async_copy(ref, ref, sem).wait()

    def push(src, dst, send, recv, where):
        pltpu.make_async_remote_copy(
            src_ref=src, dst_ref=dst, send_sem=send, recv_sem=recv, device_id=where, device_id_type=MESH
        ).start()

    def load_inverse(k):
        return pltpu.make_async_copy(inverse_ref.at[k], inv.at[k], inverse_sem.at[k])

    def load_panel(k):
        part = pl.ds(k * SLC * TILES, SLC * TILES)
        return pltpu.make_async_copy(panel_ref.at[part], flat.at[part], panel_sem.at[k])

    load_right = pltpu.make_async_copy(right_ref, right_flat, right_sem)
    load_right.start()

    @pl.when(q == 0)
    def _():
        load_inverse(0).start()

    for k in range(STEPS):
        load_panel(k).start()

    barrier = pltpu.get_barrier_semaphore()

    def hello(row, col):
        pl.semaphore_signal(barrier, inc=1, device_id=(row, col), device_id_type=MESH)

    @pl.when(q == 1)
    def _():
        hello(p, 0)

    @pl.when(is_chain | (q == 3))
    def _():
        hello(p, 1)

    @pl.when(is_chain | is_relay | (q == 3))
    def _():
        hello(p, 2)

    for r, group in RELAYS.items():

        @pl.when((q == group[0]) | (q == group[1]) | (q == group[2]) | (q == group[3]))
        def _():
            hello(p, r)

    for c in CHAIN:

        @pl.when(q != c)
        def _():
            hello(p, c)

    @pl.when((q == 2) | (q > 3))
    def _():
        hello(p, 3)

    @pl.when(q > 3)
    def _():
        def ring(i, _):
            hello(lax.rem(p + i, ROWS), q)
            return 0

        lax.fori_loop(1, ROWS, ring, 0)

    @pl.when(is_chain)
    def _():
        for k in range(1, STEPS):
            load_inverse(k).start()

    load_right.wait()
    for j in range(TILES):
        right[:, 128 * j : 128 * (j + 1)] = right_flat[pl.ds(j, RHS, stride=TILES), :]

    def panel_tile(k, j):
        return flat[pl.ds(k * SLC * TILES + j, SLC, stride=TILES), :]

    def split_block(n, tile):
        for j in range(TILES):
            at = slice(128 * j, 128 * (j + 1))
            block_high[n, :, at], block_low[n, :, at] = split(tile(j))

    own = jnp.where(p == 0, 1.0, 0.0).astype(F32)

    def send_base(k):
        for n, c in enumerate(CHAIN):
            base_out[n] = base[PART * n : PART * (n + 1), :]
            push(
                base_out.at[n],
                base_in.at[k - 1],
                base_send,
                base_recv.at[k - 1],
                (p, c),
            )

    def block(n):
        return block_high[n], block_low[n]

    @pl.when(q == 0)
    def _():
        load_inverse(0).wait()
        pieces[0, :, 0:SLC] = dot3(right[...], split(inv[0]), 1)
        pl.semaphore_wait(barrier, 1)
        push(pieces.at[0], pieces.at[0], first_send, piece_recv.at[0], (p, 1))

    @pl.when(q == 1)
    def _():
        load_panel(0).wait()
        split_block(0, lambda j: panel_tile(0, j))
        pl.semaphore_wait(barrier, len(CHAIN) + 1)
        wait(pieces.at[0], piece_recv.at[0])
        base[...] = own * right[...] - dot3(pieces[0, :, 0:SLC], block(0), 0)
        send_base(1)
        push(pieces.at[0], pieces.at[0], first_send, piece_recv.at[0], (p, 3))

    def send_block(k):
        for n in range(3):
            for r in RELAYS:
                push(
                    flat.at[pl.ds((k - 1) * SLC * TILES + n * THIRD, THIRD)],
                    rep_flat.at[k - 2, pl.ds(n * THIRD, THIRD)],
                    rep_send,
                    rep_recv.at[k - 2, n],
                    (p, r),
                )

    def hand_on(m):
        for n in range(3):
            part = rep_flat.at[m, pl.ds(n * THIRD, THIRD)]
            wait(part, rep_recv.at[m, n])
            for r, group in RELAYS.items():

                @pl.when(q == r)
                def _():
                    for c in group:
                        push(part, part, relay_send.at[m], rep_recv.at[m, n], (p, c))

    def wait_block(m):
        for n in range(3):
            wait(rep_flat.at[m, pl.ds(n * THIRD, THIRD)], rep_recv.at[m, n])

    @pl.when(q == 2)
    def _():
        load_panel(1).wait()
        pl.semaphore_wait(barrier, len(CHAIN) + len(RELAYS) + 1)
        send_block(2)
        load_panel(0).wait()
        split_block(0, lambda j: panel_tile(0, j))
        wait(pieces.at[0], piece_recv.at[0])
        base[...] = own * right[...] - dot3(pieces[0, :, 0:SLC], block(0), 0)
        send_base(2)
        wait(flat.at[pl.ds(0, 9 * THIRD)], rep_send)
        pl.semaphore_signal(rep_turn, inc=1, device_id=(p, 3), device_id_type=MESH)

    @pl.when(q == 3)
    def _():
        for k in range(2):
            load_panel(k).wait()
            split_block(k, lambda j: panel_tile(k, j))
        load_panel(2).wait()
        pl.semaphore_wait(barrier, COLS - 3)
        wait(pieces.at[0], piece_recv.at[0])
        push(pieces.at[0], pieces.at[0], first_send, piece_recv.at[0], (p, 2))

        def spread_first(i, _):
            push(pieces.at[0], pieces.at[0], piece_send.at[0], piece_recv.at[0], (p, i))
            return 0

        lax.fori_loop(4, COLS, spread_first, 0)
        base[...] = own * right[...] - dot3(pieces[0, :, 0:SLC], block(0), 0)
        pl.semaphore_wait(rep_turn, 1)
        send_block(3)

    @pl.when(is_chain)
    def _():
        pl.semaphore_wait(barrier, ROWS - 1 + COLS - 1)

    @pl.when((q > 3) & jnp.logical_not(is_chain | is_relay))
    def _():
        pl.semaphore_wait(barrier, ROWS - 1)

    @pl.when(is_relay)
    def _():
        pl.semaphore_wait(barrier, ROWS - 1 + 4)
        hand_on(0)

    lane = lax.broadcasted_iota(jnp.int32, (SLC, 128), 1)

    def cut_block(k, _):
        for n in range(ROWS):
            tile, shift = (SLC * n) // 128, (SLC * n) % 128
            value = panel_tile(k, tile)
            if shift:
                value = pltpu.roll(value, 128 - shift, 1)
                if shift > 128 - SLC:
                    after = pltpu.roll(panel_tile(k, tile + 1), 128 - shift, 1)
                    value = jnp.where(lane < 128 - shift, value, after)
            at = slice(128 * n, 128 * (n + 1))
            cut_high[k, :, at], cut_low[k, :, at] = split(value)
        return 0

    for k in range(STEPS):
        ready = {0: (1, 2, 3), 1: (2, 3), 2: (3,), 3: ()}[k]
        pending = q >= 0
        for c in ready:
            pending = pending & (q != c)

        @pl.when(pending)
        def _():
            load_panel(k).wait()

    lax.fori_loop(0, STEPS, cut_block, 0)

    def add_piece(k):
        if k:
            for n in range(len(CHAIN)):
                pieces[k, PART * n : PART * (n + 1), :] = parts[k - 1, n]
        piece = pieces[k, :, 0:SLC]
        for n in range(0, ROWS, 2):
            at = slice(128 * n, 128 * (n + 2))
            term = dot3(piece, (cut_high[k, :, at], cut_low[k, :, at]), 0)
            for h in range(2):
                value = term[:, 128 * h : 128 * (h + 1)]
                if k == 0:
                    acc[n + h] = value
                else:
                    acc[n + h] += value

    def far_first(i):
        return lax.rem(p + 8 + (1 - 2 * lax.rem(i, 2)) * lax.div(i + 1, 2), ROWS)

    @pl.when(is_chain)
    def _():
        my_cut = pl.ds(pl.multiple_of(CUT * lax.rem(p, 4), 128), CUT)

        def spread_to(k, to):
            push(mine.at[k], parts.at[k - 1, g], piece_send.at[k], piece_recv.at[k], (p, to))

        def spread(k):
            def send(i, _):
                spread_to(k, lax.rem(q + i, COLS))
                return 0

            lax.fori_loop(1, COLS, send, 0)

        def others(k):
            wait(parts.at[k - 1, pl.ds(0, len(CHAIN) - 1)], piece_recv.at[k])
            parts[k - 1, g] = mine[k]

        for k in range(1, STEPS):
            load_inverse(k).wait()
            inv_high[k], inv_low[k] = split(inv[k])

        for k in range(1, STEPS):
            wait(base_in.at[k - 1], base_recv.at[k - 1])
            if k == 1:
                rs_out[0] = base_in[0]
            else:
                rs_out[k - 1] = base_in[k - 1] - dot3(mine[k - 1, :, 0:SLC], block(k - 2), 0)

            def scatter(i, _):
                to = far_first(i)
                part = pl.ds(pl.multiple_of(CUT * lax.rem(to, 4), 128), CUT)
                slot = lax.rem(p - to + ROWS, ROWS) - 1
                push(
                    rs_out.at[k - 1, :, part],
                    rs_in.at[k - 1, slot],
                    rs_send.at[k - 1],
                    rs_recv.at[k - 1],
                    (to, q),
                )
                return 0

            lax.fori_loop(0, ROWS - 1, scatter, 0)
            if k == 1:
                wait(pieces.at[0], piece_recv.at[0])
            else:
                spread(k - 1)
                others(k - 1)
            add_piece(k - 1)

            wait(rs_in.at[k - 1], rs_recv.at[k - 1])
            total = rs_out[k - 1, :, my_cut]
            for n in range(ROWS - 1):
                total = total + rs_in[k - 1, n]
            residue[k - 1, :, my_cut] = total
            for d in (2, -1, 1):
                push(
                    residue.at[k - 1, :, my_cut],
                    residue.at[k - 1, :, my_cut],
                    ag_send.at[k - 1],
                    ag_recv.at[k - 1],
                    (lax.rem(p - d + ROWS, ROWS), q),
                )
            if k < STEPS - 1:
                wait_block(k - 1)
                split_block(k - 1, lambda j: rep_flat[k - 1, pl.ds(j, SLC, stride=TILES), :])
            wait(residue.at[k - 1, :, pl.ds(0, 3 * CUT)], ag_recv.at[k - 1])
            mine[k, :, 0:SLC] = dot3(residue[k - 1], (inv_high[k], inv_low[k]), 1)
            mine[k, :, SLC:] = jnp.zeros((PART, 128 - SLC), F32)

        last = STEPS - 1
        x, y, core = lax.div(q, 8), lax.rem(lax.div(q, 2), 4), lax.rem(q, 2)
        for dx, dy, dc in AROUND:
            to = lax.rem(x + dx, 4) * 8 + lax.rem(y + dy, 4) * 2 + lax.rem(core + dc, 2)
            spread_to(last, to)
        others(last)

    @pl.when(jnp.logical_not(is_chain))
    def _():
        @pl.when(q > 3)
        def _():
            wait(pieces.at[0], piece_recv.at[0])

        add_piece(0)

        @pl.when(is_relay)
        def _():
            hand_on(1)

        wait(parts.at[0], piece_recv.at[1])
        add_piece(1)

        @pl.when(q == 3)
        def _():
            base[...] = base[...] - dot3(pieces[1, :, 0:SLC], block(1), 0)
            send_base(3)

        wait(parts.at[1], piece_recv.at[2])
        add_piece(2)
        wait(parts.at[2], piece_recv.at[3])

    add_piece(STEPS - 1)

    wide = lax.broadcasted_iota(jnp.int32, (RHS // 4, 128), 1)
    for slot, d in enumerate(ORDER):
        n = lax.rem(p + d, ROWS)
        rest = acc[n, TAIL:RHS, :]
        for a in range(3):
            at = slice(RHS // 4 * a, RHS // 4 * (a + 1))
            packed[slot, at, :] = jnp.where(wide < SLC, acc[n, at, :], pltpu.roll(rest, SLC - 32 * a, 1))
        if slot in (3, 6):
            part = pl.ds(0, 4) if slot == 3 else pl.ds(4, 3)
            to = 1 if slot == 3 else ROWS - 1
            push(packed.at[part], near_in.at[part], near_send, near_recv, (lax.rem(p + to, ROWS), q))

    def finish(slot):
        push(
            packed.at[slot],
            far_in.at[slot - 7],
            far_send,
            far_recv,
            (lax.rem(p + ORDER[slot], ROWS), q),
        )

    finish(14)
    solved_ref[...] = pieces[:, :, 0:SLC]

    tile = lax.div(3 * p, 4)
    shift = 32 * lax.rem(3 * p, 4)
    here = right[:, pl.ds(pl.multiple_of(128 * tile, 128), 128)]
    after = right[:, pl.ds(pl.multiple_of(128 * jnp.minimum(tile + 1, TILES - 1), 128), 128)]
    turn = lax.rem(128 - shift, 128)
    lanes = lax.broadcasted_iota(jnp.int32, (RHS, 128), 1)
    total = jnp.where(lanes < 128 - shift, pltpu.roll(here, turn, 1), pltpu.roll(after, turn, 1))

    wait(near_in, near_recv)
    for slot in (10, 9, 13, 8, 12, 7, 11):
        packed[slot] = packed[slot] + near_in[slot - 7]
        finish(slot)
    term = packed[15]
    wait(far_in, far_recv)
    for n in range(8):
        term = term + far_in[n]
    acc[0] = total
    acc[1, 0:TAIL, :] = term
    updated_ref[0:TAIL, :] = (acc[1, 0:TAIL, :] - acc[0, 0:TAIL, :])[:, 0:SLC]
    last = pltpu.roll(acc[1, RHS // 2 : TAIL, :], SLC, 1)
    last = jnp.where(wide < 64, pltpu.roll(acc[1, RHS // 4 : RHS // 2, :], 64, 1), last)
    last = jnp.where(wide < 32, pltpu.roll(acc[1, 0 : RHS // 4, :], 32, 1), last)
    updated_ref[TAIL:RHS, :] = (last - acc[0, TAIL:RHS, :])[:, 0:SLC]

    wait(near_in, near_send)
    wait(far_in, far_send)

    @pl.when((q == 0) | (q == 1) | (q == 3))
    def _():
        wait(pieces.at[0], first_send)

    @pl.when((q >= 1) & (q <= 3))
    def _():
        wait(base_out, base_send)

    @pl.when(q == 3)
    def _():
        wait(flat.at[pl.ds(0, (COLS - 4) * RHS)], piece_send.at[0])
        wait(flat.at[pl.ds(0, 9 * THIRD)], rep_send)

    @pl.when(is_relay)
    def _():
        for m in range(2):
            wait(flat, relay_send.at[m])

    @pl.when(is_chain)
    def _():
        for k in range(1, STEPS):
            wait(rs_in.at[k - 1], rs_send.at[k - 1])
            wait(residue.at[k - 1, :, pl.ds(0, 3 * CUT)], ag_send.at[k - 1])
            wait(flat.at[pl.ds(0, (COLS - 1) * PART)], piece_send.at[k])


def body(panel, inverse_blocks, right_side):
    hbm = pl.BlockSpec(memory_space=pltpu.HBM)
    vmem = pl.BlockSpec(memory_space=pltpu.VMEM)
    dma = pltpu.SemaphoreType.DMA
    solved, updated = pl.pallas_call(
        kernel,
        out_shape=(
            pltpu.VMEM((STEPS, RHS, SLC), F32),
            pltpu.VMEM((RHS, SLC), F32),
        ),
        in_specs=[hbm, hbm, hbm],
        out_specs=(vmem, vmem),
        scratch_shapes=[
            pltpu.VMEM((STEPS * SLC * TILES, 128), F32),
            pltpu.VMEM((STEPS, SLC, ROWS * 128), BF16),
            pltpu.VMEM((STEPS, SLC, ROWS * 128), BF16),
            pltpu.VMEM((2, SLC * TILES, 128), F32),
            pltpu.VMEM((2, SLC, BLK), BF16),
            pltpu.VMEM((2, SLC, BLK), BF16),
            pltpu.VMEM((STEPS, SLC, BLK), F32),
            pltpu.VMEM((STEPS, SLC, BLK), BF16),
            pltpu.VMEM((STEPS, SLC, BLK), BF16),
            pltpu.VMEM((RHS * TILES, 128), F32),
            pltpu.VMEM((RHS, BLK), F32),
            pltpu.VMEM((STEPS, RHS, 128), F32),
            pltpu.VMEM((3, len(CHAIN), PART, 128), F32),
            pltpu.VMEM((RHS, BLK), F32),
            pltpu.VMEM((len(CHAIN), PART, BLK), F32),
            pltpu.VMEM((3, PART, BLK), F32),
            pltpu.VMEM((3, PART, BLK), F32),
            pltpu.VMEM((3, ROWS - 1, PART, CUT), F32),
            pltpu.VMEM((3, PART, BLK), F32),
            pltpu.VMEM((STEPS, PART, 128), F32),
            pltpu.VMEM((ROWS, RHS, 128), F32),
            pltpu.VMEM((ROWS, TAIL, 128), F32),
            pltpu.VMEM((7, TAIL, 128), F32),
            pltpu.VMEM((8, TAIL, 128), F32),
            dma((STEPS,)),
            dma((STEPS,)),
            dma,
            dma,
            dma((2, 3)),
            pltpu.SemaphoreType.REGULAR,
            dma((2,)),
            dma,
            dma((STEPS,)),
            dma((STEPS,)),
            dma,
            dma((3,)),
            dma((3,)),
            dma((3,)),
            dma((3,)),
            dma((3,)),
            dma,
            dma,
            dma,
            dma,
        ],
        compiler_params=pltpu.CompilerParams(collective_id=0, has_side_effects=True, vmem_limit_bytes=61500 * 1024),
        name="solve",
    )(
        panel.reshape(STEPS * SLC * TILES, 128),
        inverse_blocks,
        right_side.reshape(RHS * TILES, 128),
    )
    return jnp.transpose(solved, (1, 0, 2)), -updated.reshape(RHS, 1, 1, SLC)


def solution(mesh):
    placed = (P(None, "row", None, "col", None), P(None, "row", None), P(None, None, "col", None))
    return jax.shard_map(
        body,
        mesh=mesh,
        in_specs=placed,
        out_specs=(P(None, None, "row"), P(None, None, "col", "row")),
        check_vma=False,
    )
```

```python
import jax
import jax.numpy as jnp
from jax import lax
from jax.experimental import pallas as pl
from jax.experimental.pallas import tpu as pltpu
from jax.sharding import PartitionSpec as P

MESH = pl.DeviceIdType.MESH
F32 = jnp.float32
BF16 = jnp.bfloat16
ROWS, COLS = 16, 32
STEPS, RHS, BLK, SLC = 4, 48, 1536, 96
TILES = BLK // 128
CHAIN = (4, 6, 8, 10, 12, 14, 16, 18, 24, 26, 28, 30)
RELAYS = {5: (4, 6, 14, 30), 11: (10, 8, 12, 18), 27: (26, 24, 28, 16)}
THIRD = SLC * BLK // 128 // 3
PART = RHS // len(CHAIN)
CUT = BLK // 4
AROUND = sorted(
    [(x, y, c) for x in range(4) for y in range(4) for c in range(2) if x or y or c],
    key=lambda d: (-min(d[0], 4 - d[0]) - min(d[1], 4 - d[1]), d),
)
TAIL = RHS - RHS // 4
HALF = ROWS // 2 * 128


def split(value):
    high = value.astype(BF16)
    return high, (value - high.astype(F32)).astype(BF16)


def dot3(left, right, axis):
    rows = left.shape[0]
    high = left.astype(BF16)
    wide = high.astype(F32)
    stacked = jnp.concatenate([wide, left - wide], 0).astype(BF16)
    dims = (((1,), (axis,)), ((), ()))
    both = lax.dot_general(stacked, right[0], dims, preferred_element_type=F32)
    rest = lax.dot_general(high, right[1], dims, preferred_element_type=F32)
    return both[:rows] + (both[rows:] + rest)


def kernel(
    panel_ref,
    inverse_ref,
    right_ref,
    solved_ref,
    updated_ref,
    flat,
    cut_high,
    cut_low,
    rep_flat,
    block_high,
    block_low,
    inv,
    inv_high,
    inv_low,
    right_flat,
    right,
    pieces,
    parts,
    last_parts,
    last_mine,
    give,
    taken,
    inv_other,
    last_high,
    last_low,
    base,
    base_out,
    base_in,
    rs_out,
    rs_in,
    residue,
    mine,
    acc,
    packed,
    near_out,
    near_in,
    far_in,
    panel_sem,
    inverse_sem,
    right_sem,
    rep_send,
    rep_recv,
    rep_turn,
    relay_send,
    first_send,
    piece_send,
    piece_recv,
    base_send,
    base_recv,
    rs_send,
    rs_recv,
    ag_send,
    ag_recv,
    give_send,
    give_recv,
    other_send,
    other_recv,
    near_send,
    near_recv,
    far_send,
    far_recv,
):
    p = lax.axis_index("row")
    q = lax.axis_index("col")
    is_chain = (lax.rem(q, 2) == 0) & (q > 3) & (q != 20) & (q != 22)
    g = jnp.where(q < 20, lax.div(q - 4, 2), lax.div(q - 8, 2))
    is_relay = (q == 5) | (q == 11) | (q == 27)
    pair = p + 1 - 2 * lax.rem(p, 2)

    def wait(ref, sem):
        pltpu.make_async_copy(ref, ref, sem).wait()

    def push(src, dst, send, recv, where):
        pltpu.make_async_remote_copy(
            src_ref=src, dst_ref=dst, send_sem=send, recv_sem=recv, device_id=where, device_id_type=MESH
        ).start()

    def load_inverse(k):
        return pltpu.make_async_copy(inverse_ref.at[k], inv.at[k], inverse_sem.at[k])

    def load_panel(k):
        part = pl.ds(k * SLC * TILES, SLC * TILES)
        return pltpu.make_async_copy(panel_ref.at[part], flat.at[part], panel_sem.at[k])

    load_right = pltpu.make_async_copy(right_ref, right_flat, right_sem)
    load_right.start()

    @pl.when(q == 0)
    def _():
        load_inverse(0).start()

    for k in range(STEPS):
        load_panel(k).start()

    barrier = pltpu.get_barrier_semaphore()

    def hello(row, col):
        pl.semaphore_signal(barrier, inc=1, device_id=(row, col), device_id_type=MESH)

    @pl.when(q == 1)
    def _():
        hello(p, 0)

    @pl.when(is_chain | (q == 3))
    def _():
        hello(p, 1)

    @pl.when(is_chain | is_relay | (q == 3))
    def _():
        hello(p, 2)

    for r, group in RELAYS.items():

        @pl.when((q == group[0]) | (q == group[1]) | (q == group[2]) | (q == group[3]))
        def _():
            hello(p, r)

    for c in CHAIN:

        @pl.when(q != c)
        def _():
            hello(p, c)

    @pl.when((q == 2) | (q > 3))
    def _():
        hello(p, 3)

    @pl.when(q == 3)
    def _():
        hello(pair, 3)

    @pl.when(q > 3)
    def _():
        def ring(i, _):
            hello(lax.rem(p + i, ROWS), q)
            return 0

        lax.fori_loop(1, ROWS, ring, 0)

    @pl.when(is_chain)
    def _():
        for k in range(1, STEPS):
            load_inverse(k).start()

    load_right.wait()
    for j in range(TILES):
        right[:, 128 * j : 128 * (j + 1)] = right_flat[pl.ds(j, RHS, stride=TILES), :]

    def panel_tile(k, j):
        return flat[pl.ds(k * SLC * TILES + j, SLC, stride=TILES), :]

    def split_block(n, tile):
        for j in range(TILES):
            at = slice(128 * j, 128 * (j + 1))
            block_high[n, :, at], block_low[n, :, at] = split(tile(j))

    own = jnp.where(p == 0, 1.0, 0.0).astype(F32)

    def send_base(k):
        for n, c in enumerate(CHAIN):
            base_out[n] = base[PART * n : PART * (n + 1), :]
            push(
                base_out.at[n],
                base_in.at[k - 1],
                base_send,
                base_recv.at[k - 1],
                (p, c),
            )

    def block(n):
        return block_high[n], block_low[n]

    @pl.when(q == 0)
    def _():
        load_inverse(0).wait()
        pieces[0, :, 0:SLC] = dot3(right[...], split(inv[0]), 1)
        pl.semaphore_wait(barrier, 1)
        push(pieces.at[0], pieces.at[0], first_send, piece_recv.at[0], (p, 1))

    @pl.when(q == 1)
    def _():
        load_panel(0).wait()
        split_block(0, lambda j: panel_tile(0, j))
        pl.semaphore_wait(barrier, len(CHAIN) + 1)
        wait(pieces.at[0], piece_recv.at[0])
        base[...] = own * right[...] - dot3(pieces[0, :, 0:SLC], block(0), 0)
        send_base(1)
        push(pieces.at[0], pieces.at[0], first_send, piece_recv.at[0], (p, 3))

    def send_block(k):
        for n in range(3):
            for r in RELAYS:
                push(
                    flat.at[pl.ds((k - 1) * SLC * TILES + n * THIRD, THIRD)],
                    rep_flat.at[k - 2, pl.ds(n * THIRD, THIRD)],
                    rep_send,
                    rep_recv.at[k - 2, n],
                    (p, r),
                )

    def hand_on(m):
        for n in range(3):
            part = rep_flat.at[m, pl.ds(n * THIRD, THIRD)]
            wait(part, rep_recv.at[m, n])
            for r, group in RELAYS.items():

                @pl.when(q == r)
                def _():
                    for c in group:
                        push(part, part, relay_send.at[m], rep_recv.at[m, n], (p, c))

    def wait_block(m):
        for n in range(3):
            wait(rep_flat.at[m, pl.ds(n * THIRD, THIRD)], rep_recv.at[m, n])

    @pl.when(q == 2)
    def _():
        load_panel(1).wait()
        pl.semaphore_wait(barrier, len(CHAIN) + len(RELAYS) + 1)
        send_block(2)
        load_panel(0).wait()
        split_block(0, lambda j: panel_tile(0, j))
        wait(pieces.at[0], piece_recv.at[0])
        base[...] = own * right[...] - dot3(pieces[0, :, 0:SLC], block(0), 0)
        send_base(2)
        wait(flat.at[pl.ds(0, 9 * THIRD)], rep_send)
        pl.semaphore_signal(rep_turn, inc=1, device_id=(p, 3), device_id_type=MESH)

    @pl.when(q == 3)
    def _():
        for k in range(2):
            load_panel(k).wait()
            split_block(k, lambda j: panel_tile(k, j))
        load_panel(2).wait()
        pl.semaphore_wait(barrier, COLS - 3 + 1)
        wait(pieces.at[0], piece_recv.at[0])
        push(pieces.at[0], pieces.at[0], first_send, piece_recv.at[0], (p, 2))

        def spread_first(i, _):
            push(pieces.at[0], pieces.at[0], piece_send.at[0], piece_recv.at[0], (p, i))
            return 0

        lax.fori_loop(4, COLS, spread_first, 0)
        base[...] = own * right[...] - dot3(pieces[0, :, 0:SLC], block(0), 0)
        pl.semaphore_wait(rep_turn, 1)
        send_block(3)

    @pl.when(is_chain)
    def _():
        pl.semaphore_wait(barrier, ROWS - 1 + COLS - 1)

    @pl.when((q > 3) & jnp.logical_not(is_chain | is_relay))
    def _():
        pl.semaphore_wait(barrier, ROWS - 1)

    @pl.when(is_relay)
    def _():
        pl.semaphore_wait(barrier, ROWS - 1 + 4)
        hand_on(0)

    lane = lax.broadcasted_iota(jnp.int32, (SLC, 128), 1)

    def cut_tile(k, slot):
        n = lax.rem((p if slot < ROWS // 2 else pair) + 2 * slot, ROWS)
        tile, shift = lax.div(3 * n, 4), 32 * lax.rem(3 * n, 4)
        turn = lax.rem(128 - shift, 128)
        value = pltpu.roll(panel_tile(k, tile), turn, 1)
        after = pltpu.roll(panel_tile(k, jnp.minimum(tile + 1, TILES - 1)), turn, 1)
        return jnp.where(lane < 128 - shift, value, after)

    def cut_block(k, _):
        for n in range(ROWS):
            at = slice(128 * n, 128 * (n + 1))
            cut_high[k, :, at], cut_low[k, :, at] = split(cut_tile(k, n))
        return 0

    def cut_last():
        for n in range(ROWS // 2):
            at = slice(128 * n, 128 * (n + 1))
            cut_high[STEPS - 1, :, at], cut_low[STEPS - 1, :, at] = split(cut_tile(STEPS - 1, n))
            give[:, at] = cut_tile(STEPS - 1, ROWS // 2 + n)

    def exchange_last():
        push(give, taken, give_send, give_recv, (pair, q))

    def take_last():
        wait(taken, give_recv)
        cut_high[STEPS - 1, :, HALF:], cut_low[STEPS - 1, :, HALF:] = split(taken[...])

    for k in range(STEPS):
        ready = {0: (1, 2, 3), 1: (2, 3), 2: (3,), 3: ()}[k]
        pending = q >= 0
        for c in ready:
            pending = pending & (q != c)

        @pl.when(pending)
        def _():
            load_panel(k).wait()

    cut_last()

    @pl.when((q > 2) & jnp.logical_not(is_chain))
    def _():
        exchange_last()

    lax.fori_loop(0, STEPS - 1, cut_block, 0)

    def add_piece(k):
        if k:
            for n in range(len(CHAIN)):
                pieces[k, PART * n : PART * (n + 1), :] = parts[k - 1, n]
        piece = pieces[k, :, 0:SLC]
        for n in range(0, ROWS, 2):
            at = slice(128 * n, 128 * (n + 2))
            term = dot3(piece, (cut_high[k, :, at], cut_low[k, :, at]), 0)
            for h in range(2):
                value = term[:, 128 * h : 128 * (h + 1)]
                if k == 0:
                    acc[n + h] = value
                else:
                    acc[n + h] += value

    wide = lax.broadcasted_iota(jnp.int32, (RHS // 4, 128), 1)

    def pack(slot, put):
        rest = acc[slot, TAIL:RHS, :]
        for a in range(3):
            at = slice(RHS // 4 * a, RHS // 4 * (a + 1))
            put(at, jnp.where(wide < SLC, acc[slot, at, :], pltpu.roll(rest, SLC - 32 * a, 1)))

    def exchange_sums():
        for n in range(ROWS // 2):

            def put(at, value):
                near_out[n, at, :] = value

            pack(ROWS // 2 + n, put)
        push(near_out, near_in, near_send, near_recv, (pair, q))

    def far_first(i):
        return lax.rem(p + 8 + (1 - 2 * lax.rem(i, 2)) * lax.div(i + 1, 2), ROWS)

    @pl.when(is_chain)
    def _():
        my_cut = pl.ds(pl.multiple_of(CUT * lax.rem(p, 4), 128), CUT)

        def spread_to(k, to):
            if k == STEPS - 1:
                src, dst = last_mine, last_parts.at[g]
            else:
                src, dst = mine.at[k], parts.at[k - 1, g]
            push(src, dst, piece_send.at[k], piece_recv.at[k], (p, to))

        def spread(k):
            def send(i, _):
                spread_to(k, lax.rem(q + i, COLS))
                return 0

            lax.fori_loop(1, COLS, send, 0)

        def others(k):
            wait(parts.at[k - 1, pl.ds(0, len(CHAIN) - 1)], piece_recv.at[k])
            parts[k - 1, g] = mine[k]

        for k in range(1, STEPS):
            load_inverse(k).wait()
            if k < STEPS - 1:
                inv_high[k], inv_low[k] = split(inv[k])
        none = jnp.zeros((128 - SLC, BLK), BF16)
        for ref, value in zip((last_high, last_low), split(inv[STEPS - 1])):
            ref[0:SLC, :] = value
            ref[SLC:128, :] = none
            ref[128 + SLC :, :] = none

        for k in range(1, STEPS):
            wait(base_in.at[k - 1], base_recv.at[k - 1])
            if k == 1:
                rs_out[0] = base_in[0]
            else:
                rs_out[k - 1] = base_in[k - 1] - dot3(mine[k - 1, :, 0:SLC], block(k - 2), 0)

            def scatter(i, _):
                to = far_first(i)
                part = pl.ds(pl.multiple_of(CUT * lax.rem(to, 4), 128), CUT)
                slot = lax.rem(p - to + ROWS, ROWS) - 1
                push(
                    rs_out.at[k - 1, :, part],
                    rs_in.at[k - 1, slot],
                    rs_send.at[k - 1],
                    rs_recv.at[k - 1],
                    (to, q),
                )
                return 0

            lax.fori_loop(0, ROWS - 1, scatter, 0)
            if k == 1:
                exchange_last()
            if k == 2:
                push(inv.at[STEPS - 1], inv_other, other_send, other_recv, (pair, q))
            if k == 1:
                wait(pieces.at[0], piece_recv.at[0])
            else:
                spread(k - 1)
                others(k - 1)
            add_piece(k - 1)
            if k == STEPS - 1:
                exchange_sums()
                wait(inv_other, other_recv)
                last_high[128 : 128 + SLC, :], last_low[128 : 128 + SLC, :] = split(inv_other[...])
                take_last()

            wait(rs_in.at[k - 1], rs_recv.at[k - 1])
            total = rs_out[k - 1, :, my_cut]
            for n in range(ROWS - 1):
                total = total + rs_in[k - 1, n]
            residue[k - 1, :, my_cut] = total
            for d in (2, -1, 1):
                push(
                    residue.at[k - 1, :, my_cut],
                    residue.at[k - 1, :, my_cut],
                    ag_send.at[k - 1],
                    ag_recv.at[k - 1],
                    (lax.rem(p - d + ROWS, ROWS), q),
                )
            if k < STEPS - 1:
                wait_block(k - 1)
                split_block(k - 1, lambda j: rep_flat[k - 1, pl.ds(j, SLC, stride=TILES), :])
            wait(residue.at[k - 1, :, pl.ds(0, 3 * CUT)], ag_recv.at[k - 1])
            if k < STEPS - 1:
                mine[k, :, 0:SLC] = dot3(residue[k - 1], (inv_high[k], inv_low[k]), 1)
                mine[k, :, SLC:] = jnp.zeros((PART, 128 - SLC), F32)
            else:
                both = dot3(residue[k - 1], (last_high[...], last_low[...]), 1)
                last_mine[0] = both[:, :128]
                last_mine[1] = both[:, 128:]

        last = STEPS - 1
        x, y, core = lax.div(q, 8), lax.rem(lax.div(q, 2), 4), lax.rem(q, 2)
        for dx, dy, dc in AROUND:
            to = lax.rem(x + dx, 4) * 8 + lax.rem(y + dy, 4) * 2 + lax.rem(core + dc, 2)
            spread_to(last, to)
        wait(last_parts.at[pl.ds(0, len(CHAIN) - 1)], piece_recv.at[last])
        last_parts[g] = last_mine[...]

    @pl.when(jnp.logical_not(is_chain))
    def _():
        @pl.when(q > 3)
        def _():
            wait(pieces.at[0], piece_recv.at[0])

        add_piece(0)

        @pl.when(is_relay)
        def _():
            hand_on(1)

        wait(parts.at[0], piece_recv.at[1])
        add_piece(1)

        @pl.when(q == 3)
        def _():
            base[...] = base[...] - dot3(pieces[1, :, 0:SLC], block(1), 0)
            send_base(3)

        wait(parts.at[1], piece_recv.at[2])
        add_piece(2)
        exchange_sums()

        @pl.when(q > 2)
        def _():
            take_last()

        @pl.when(q < 3)
        def _():
            none = jnp.zeros((SLC, HALF), BF16)
            cut_high[STEPS - 1, :, HALF:] = none
            cut_low[STEPS - 1, :, HALF:] = none

        wait(last_parts, piece_recv.at[3])

    wait(near_in, near_recv)
    for n in range(len(CHAIN)):
        pieces[STEPS - 1, PART * n : PART * (n + 1), :] = last_parts[n, 0]
        pieces[STEPS, PART * n : PART * (n + 1), :] = last_parts[n, 1]
    for n in (4, 2, 6, 0):
        at, to = slice(128 * n, 128 * (n + 2)), slice(HALF + 128 * n, HALF + 128 * (n + 2))
        term = dot3(pieces[STEPS - 1, :, 0:SLC], (cut_high[STEPS - 1, :, at], cut_low[STEPS - 1, :, at]), 0)
        term = term + dot3(pieces[STEPS, :, 0:SLC], (cut_high[STEPS - 1, :, to], cut_low[STEPS - 1, :, to]), 0)
        for slot in (n, n + 1):
            acc[slot] += term[:, 128 * (slot - n) : 128 * (slot - n + 1)]

            def put(at, value):
                packed[slot, at, :] = value + near_in[slot, at, :]

            pack(slot, put)
            if slot:
                push(
                    packed.at[slot],
                    far_in.at[slot - 1],
                    far_send,
                    far_recv,
                    (lax.rem(p + 2 * slot, ROWS), q),
                )

    solved_ref[...] = pieces[0:STEPS, :, 0:SLC]

    tile = lax.div(3 * p, 4)
    shift = 32 * lax.rem(3 * p, 4)
    here = right[:, pl.ds(pl.multiple_of(128 * tile, 128), 128)]
    after = right[:, pl.ds(pl.multiple_of(128 * jnp.minimum(tile + 1, TILES - 1), 128), 128)]
    turn = lax.rem(128 - shift, 128)
    lanes = lax.broadcasted_iota(jnp.int32, (RHS, 128), 1)
    total = jnp.where(lanes < 128 - shift, pltpu.roll(here, turn, 1), pltpu.roll(after, turn, 1))

    term = packed[0]
    wait(far_in, far_recv)
    for n in range(ROWS // 2 - 1):
        term = term + far_in[n]
    acc[0] = total
    acc[1, 0:TAIL, :] = term
    updated_ref[0:TAIL, :] = (acc[1, 0:TAIL, :] - acc[0, 0:TAIL, :])[:, 0:SLC]
    last = pltpu.roll(acc[1, RHS // 2 : TAIL, :], SLC, 1)
    last = jnp.where(wide < 64, pltpu.roll(acc[1, RHS // 4 : RHS // 2, :], 64, 1), last)
    last = jnp.where(wide < 32, pltpu.roll(acc[1, 0 : RHS // 4, :], 32, 1), last)
    updated_ref[TAIL:RHS, :] = (last - acc[0, TAIL:RHS, :])[:, 0:SLC]

    wait(near_out, near_send)
    wait(far_in, far_send)

    @pl.when(q > 2)
    def _():
        wait(give, give_send)

    @pl.when((q == 0) | (q == 1) | (q == 3))
    def _():
        wait(pieces.at[0], first_send)

    @pl.when((q >= 1) & (q <= 3))
    def _():
        wait(base_out, base_send)

    @pl.when(q == 3)
    def _():
        wait(flat.at[pl.ds(0, (COLS - 4) * RHS)], piece_send.at[0])
        wait(flat.at[pl.ds(0, 9 * THIRD)], rep_send)

    @pl.when(is_relay)
    def _():
        for m in range(2):
            wait(flat, relay_send.at[m])

    @pl.when(is_chain)
    def _():
        for k in range(1, STEPS):
            wait(rs_in.at[k - 1], rs_send.at[k - 1])
            wait(residue.at[k - 1, :, pl.ds(0, 3 * CUT)], ag_send.at[k - 1])
            wait(flat.at[pl.ds(0, (COLS - 1) * PART * (2 if k == STEPS - 1 else 1))], piece_send.at[k])
        wait(inv_other, other_send)


def body(panel, inverse_blocks, right_side):
    hbm = pl.BlockSpec(memory_space=pltpu.HBM)
    vmem = pl.BlockSpec(memory_space=pltpu.VMEM)
    dma = pltpu.SemaphoreType.DMA
    solved, updated = pl.pallas_call(
        kernel,
        out_shape=(
            pltpu.VMEM((STEPS, RHS, SLC), F32),
            pltpu.VMEM((RHS, SLC), F32),
        ),
        in_specs=[hbm, hbm, hbm],
        out_specs=(vmem, vmem),
        scratch_shapes=[
            pltpu.VMEM((STEPS * SLC * TILES, 128), F32),
            pltpu.VMEM((STEPS, SLC, ROWS * 128), BF16),
            pltpu.VMEM((STEPS, SLC, ROWS * 128), BF16),
            pltpu.VMEM((2, SLC * TILES, 128), F32),
            pltpu.VMEM((2, SLC, BLK), BF16),
            pltpu.VMEM((2, SLC, BLK), BF16),
            pltpu.VMEM((STEPS, SLC, BLK), F32),
            pltpu.VMEM((STEPS, SLC, BLK), BF16),
            pltpu.VMEM((STEPS, SLC, BLK), BF16),
            pltpu.VMEM((RHS * TILES, 128), F32),
            pltpu.VMEM((RHS, BLK), F32),
            pltpu.VMEM((STEPS + 1, RHS, 128), F32),
            pltpu.VMEM((2, len(CHAIN), PART, 128), F32),
            pltpu.VMEM((len(CHAIN), 2, PART, 128), F32),
            pltpu.VMEM((2, PART, 128), F32),
            pltpu.VMEM((SLC, HALF), F32),
            pltpu.VMEM((SLC, HALF), F32),
            pltpu.VMEM((SLC, BLK), F32),
            pltpu.VMEM((256, BLK), BF16),
            pltpu.VMEM((256, BLK), BF16),
            pltpu.VMEM((RHS, BLK), F32),
            pltpu.VMEM((len(CHAIN), PART, BLK), F32),
            pltpu.VMEM((3, PART, BLK), F32),
            pltpu.VMEM((3, PART, BLK), F32),
            pltpu.VMEM((3, ROWS - 1, PART, CUT), F32),
            pltpu.VMEM((3, PART, BLK), F32),
            pltpu.VMEM((STEPS, PART, 128), F32),
            pltpu.VMEM((ROWS, RHS, 128), F32),
            pltpu.VMEM((ROWS // 2, TAIL, 128), F32),
            pltpu.VMEM((ROWS // 2, TAIL, 128), F32),
            pltpu.VMEM((ROWS // 2, TAIL, 128), F32),
            pltpu.VMEM((ROWS // 2 - 1, TAIL, 128), F32),
            dma((STEPS,)),
            dma((STEPS,)),
            dma,
            dma,
            dma((2, 3)),
            pltpu.SemaphoreType.REGULAR,
            dma((2,)),
            dma,
            dma((STEPS,)),
            dma((STEPS,)),
            dma,
            dma((3,)),
            dma((3,)),
            dma((3,)),
            dma((3,)),
            dma((3,)),
            dma,
            dma,
            dma,
            dma,
            dma,
            dma,
            dma,
            dma,
        ],
        compiler_params=pltpu.CompilerParams(collective_id=0, has_side_effects=True, vmem_limit_bytes=61500 * 1024),
        name="solve",
    )(
        panel.reshape(STEPS * SLC * TILES, 128),
        inverse_blocks,
        right_side.reshape(RHS * TILES, 128),
    )
    return jnp.transpose(solved, (1, 0, 2)), -updated.reshape(RHS, 1, 1, SLC)


def solution(mesh):
    placed = (P(None, "row", None, "col", None), P(None, "row", None), P(None, None, "col", None))
    return jax.shard_map(
        body,
        mesh=mesh,
        in_specs=placed,
        out_specs=(P(None, None, "row"), P(None, None, "col", "row")),
        check_vma=False,
    )
```

```python
import jax
import jax.numpy as jnp
from jax import lax
from jax.experimental import pallas as pl
from jax.experimental.pallas import tpu as pltpu
from jax.sharding import PartitionSpec as P

MESH = pl.DeviceIdType.MESH
F32 = jnp.float32
BF16 = jnp.bfloat16
ROWS, COLS = 16, 32
STEPS, RHS, BLK, SLC = 4, 48, 1536, 96
TILES = BLK // 128
CHAIN = (4, 6, 8, 10, 12, 14, 16, 18, 24, 26, 28, 30)
RELAYS = {5: (4, 6, 14, 30), 11: (10, 8, 12, 18), 27: (26, 24, 28, 16)}
THIRD = SLC * BLK // 128 // 3
PART = RHS // len(CHAIN)
CUT = BLK // 4
AROUND = sorted(
    [(x, y, c) for x in range(4) for y in range(4) for c in range(2) if x or y or c],
    key=lambda d: (-min(d[0], 4 - d[0]) - min(d[1], 4 - d[1]), d),
)
TAIL = RHS - RHS // 4
HALF = ROWS // 2 * 128


def hops(first, second):
    total = 0
    for a, b in ((first // 8, second // 8), (first // 2 % 4, second // 2 % 4)):
        total += min(abs(a - b), 4 - abs(a - b))
    return total


def split(value):
    high = value.astype(BF16)
    return high, (value - high.astype(F32)).astype(BF16)


def dot3(left, right, axis):
    rows = left.shape[0]
    high = left.astype(BF16)
    wide = high.astype(F32)
    stacked = jnp.concatenate([wide, left - wide], 0).astype(BF16)
    dims = (((1,), (axis,)), ((), ()))
    both = lax.dot_general(stacked, right[0], dims, preferred_element_type=F32)
    rest = lax.dot_general(high, right[1], dims, preferred_element_type=F32)
    return both[:rows] + (both[rows:] + rest)


def kernel(
    panel_ref,
    inverse_ref,
    right_ref,
    solved_ref,
    updated_ref,
    flat,
    cut_high,
    cut_low,
    rep_flat,
    block_high,
    block_low,
    inv,
    inv_high,
    inv_low,
    right_flat,
    right,
    pieces,
    parts,
    end_high,
    end_low,
    end_piece,
    last_parts,
    last_mine,
    give,
    taken,
    inv_other,
    last_high,
    last_low,
    base,
    base_out,
    base_in,
    rs_out,
    rs_in,
    residue,
    mine,
    acc,
    packed,
    near_out,
    near_in,
    far_in,
    panel_sem,
    inverse_sem,
    right_sem,
    rep_send,
    rep_recv,
    rep_turn,
    relay_send,
    first_send,
    piece_send,
    piece_recv,
    base_send,
    base_recv,
    rs_send,
    rs_recv,
    ag_send,
    ag_recv,
    give_send,
    give_recv,
    other_send,
    other_recv,
    near_send,
    near_recv,
    far_send,
    far_recv,
):
    p = lax.axis_index("row")
    q = lax.axis_index("col")
    is_chain = (lax.rem(q, 2) == 0) & (q > 3) & (q != 20) & (q != 22)
    g = jnp.where(q < 20, lax.div(q - 4, 2), lax.div(q - 8, 2))
    is_relay = (q == 5) | (q == 11) | (q == 27)
    is_beside = (lax.rem(q, 2) == 1) & (q > 3) & (q != 21) & (q != 23)
    side = 2 * lax.rem(p, 2) - 1
    pair = p - side

    def target(slot):
        return lax.rem(p + side * slot + ROWS, ROWS)


    def wait(ref, sem):
        pltpu.make_async_copy(ref, ref, sem).wait()

    def push(src, dst, send, recv, where):
        pltpu.make_async_remote_copy(
            src_ref=src, dst_ref=dst, send_sem=send, recv_sem=recv, device_id=where, device_id_type=MESH
        ).start()

    def load_inverse(k):
        return pltpu.make_async_copy(inverse_ref.at[k], inv.at[k], inverse_sem.at[k])

    def load_panel(k):
        part = pl.ds(k * SLC * TILES, SLC * TILES)
        return pltpu.make_async_copy(panel_ref.at[part], flat.at[part], panel_sem.at[k])

    load_right = pltpu.make_async_copy(right_ref, right_flat, right_sem)
    load_right.start()

    @pl.when(q == 0)
    def _():
        load_inverse(0).start()

    for k in range(STEPS):
        load_panel(k).start()

    barrier = pltpu.get_barrier_semaphore()

    def hello(row, col):
        pl.semaphore_signal(barrier, inc=1, device_id=(row, col), device_id_type=MESH)

    @pl.when(q == 1)
    def _():
        hello(p, 0)

    @pl.when(is_chain | (q == 3))
    def _():
        hello(p, 1)

    @pl.when(is_chain)
    def _():
        def ring(i, _):
            hello(lax.rem(p + 8 + (1 - 2 * lax.rem(i, 2)) * lax.div(i + 1, 2), ROWS), q)
            return 0

        lax.fori_loop(0, ROWS - 1, ring, 0)
        hello(pair, q + 1)

    @pl.when((q > 2) & jnp.logical_not(is_chain))
    def _():
        hello(pair, q)

    @pl.when(is_chain | is_relay | (q == 3))
    def _():
        hello(p, 2)

    for r, group in RELAYS.items():

        @pl.when((q == group[0]) | (q == group[1]) | (q == group[2]) | (q == group[3]))
        def _():
            hello(p, r)

    for c in CHAIN:

        @pl.when(q != c)
        def _():
            hello(p, c)

    @pl.when((q == 2) | (q > 3))
    def _():
        hello(p, 3)

    @pl.when(is_chain)
    def _():
        for k in range(1, STEPS):
            load_inverse(k).start()

    load_right.wait()
    for j in range(TILES):
        right[:, 128 * j : 128 * (j + 1)] = right_flat[pl.ds(j, RHS, stride=TILES), :]

    def panel_tile(k, j):
        return flat[pl.ds(k * SLC * TILES + j, SLC, stride=TILES), :]

    def split_block(n, tile):
        for j in range(TILES):
            at = slice(128 * j, 128 * (j + 1))
            block_high[n, :, at], block_low[n, :, at] = split(tile(j))

    own = jnp.where(p == 0, 1.0, 0.0).astype(F32)

    def send_base(k):
        for n, c in sorted(enumerate(CHAIN), key=lambda v: -hops(v[1], k)):
            base_out[n] = base[PART * n : PART * (n + 1), :]
            push(
                base_out.at[n],
                base_in.at[k - 1],
                base_send,
                base_recv.at[k - 1],
                (p, c),
            )

    def block(n):
        return block_high[n], block_low[n]

    @pl.when(q == 0)
    def _():
        load_inverse(0).wait()
        pieces[0, :, 0:SLC] = dot3(right[...], split(inv[0]), 1)
        pl.semaphore_wait(barrier, 1)
        push(pieces.at[0], pieces.at[0], first_send, piece_recv.at[0], (p, 1))

    @pl.when(q == 1)
    def _():
        load_panel(0).wait()
        split_block(0, lambda j: panel_tile(0, j))
        pl.semaphore_wait(barrier, len(CHAIN) + 1)
        wait(pieces.at[0], piece_recv.at[0])
        base[...] = own * right[...] - dot3(pieces[0, :, 0:SLC], block(0), 0)
        send_base(1)
        push(pieces.at[0], pieces.at[0], first_send, piece_recv.at[0], (p, 3))

    def send_block(k):
        for n in range(3):
            for r in RELAYS:
                push(
                    flat.at[pl.ds((k - 1) * SLC * TILES + n * THIRD, THIRD)],
                    rep_flat.at[k - 2, pl.ds(n * THIRD, THIRD)],
                    rep_send,
                    rep_recv.at[k - 2, n],
                    (p, r),
                )

    def hand_on(m):
        for n in range(3):
            part = rep_flat.at[m, pl.ds(n * THIRD, THIRD)]
            wait(part, rep_recv.at[m, n])
            for r, group in RELAYS.items():

                @pl.when(q == r)
                def _():
                    for c in group:
                        push(part, part, relay_send.at[m], rep_recv.at[m, n], (p, c))

    def wait_block(m):
        for n in range(3):
            wait(rep_flat.at[m, pl.ds(n * THIRD, THIRD)], rep_recv.at[m, n])

    @pl.when(q == 2)
    def _():
        load_panel(1).wait()
        pl.semaphore_wait(barrier, len(CHAIN) + len(RELAYS) + 1)
        send_block(2)
        load_panel(0).wait()
        split_block(0, lambda j: panel_tile(0, j))
        wait(pieces.at[0], piece_recv.at[0])
        base[...] = own * right[...] - dot3(pieces[0, :, 0:SLC], block(0), 0)
        send_base(2)
        wait(flat.at[pl.ds(0, 9 * THIRD)], rep_send)
        pl.semaphore_signal(rep_turn, inc=1, device_id=(p, 3), device_id_type=MESH)

    @pl.when(q == 3)
    def _():
        for k in range(2):
            load_panel(k).wait()
            split_block(k, lambda j: panel_tile(k, j))
        load_panel(2).wait()
        pl.semaphore_wait(barrier, COLS - 3 + 1)
        wait(pieces.at[0], piece_recv.at[0])
        push(pieces.at[0], pieces.at[0], first_send, piece_recv.at[0], (p, 2))

        def spread_first(i, _):
            push(pieces.at[0], pieces.at[0], piece_send.at[0], piece_recv.at[0], (p, i))
            return 0

        lax.fori_loop(4, COLS, spread_first, 0)
        base[...] = own * right[...] - dot3(pieces[0, :, 0:SLC], block(0), 0)
        pl.semaphore_wait(rep_turn, 1)
        send_block(3)

    @pl.when(is_chain)
    def _():
        pl.semaphore_wait(barrier, ROWS - 1 + COLS - 1)

    @pl.when((q > 3) & jnp.logical_not(is_chain | is_beside))
    def _():
        pl.semaphore_wait(barrier, 1)

    @pl.when(is_beside & jnp.logical_not(is_relay))
    def _():
        pl.semaphore_wait(barrier, 2)

    @pl.when(is_relay)
    def _():
        pl.semaphore_wait(barrier, 2 + 4)

    @pl.when(is_beside)
    def _():
        push(inverse_ref.at[STEPS - 1], inv_other, other_send, other_recv, (pair, q - 1))

    lane = lax.broadcasted_iota(jnp.int32, (SLC, 128), 1)

    def cut_tile(k, slot):
        n = target(slot) if slot < ROWS // 2 else lax.rem(pair - side * (slot - ROWS // 2) + ROWS, ROWS)
        tile, shift = lax.div(3 * n, 4), 32 * lax.rem(3 * n, 4)
        turn = lax.rem(128 - shift, 128)
        value = pltpu.roll(panel_tile(k, tile), turn, 1)
        after = pltpu.roll(panel_tile(k, jnp.minimum(tile + 1, TILES - 1)), turn, 1)
        return jnp.where(lane < 128 - shift, value, after)

    def cut_block(k, _):
        for n in range(ROWS):
            at = slice(128 * n, 128 * (n + 1))
            cut_high[k, :, at], cut_low[k, :, at] = split(cut_tile(k, n))
        return 0

    def cut_last():
        none = jnp.zeros((128 - SLC, HALF), BF16)
        for ref in (end_high, end_low):
            ref[SLC:128, :] = none
            ref[128 + SLC :, :] = none
        for n in range(ROWS // 2):
            at = slice(128 * n, 128 * (n + 1))
            end_high[0:SLC, at], end_low[0:SLC, at] = split(cut_tile(STEPS - 1, n))
            give[:, at] = cut_tile(STEPS - 1, ROWS // 2 + n)

    def exchange_last():
        push(give, taken, give_send, give_recv, (pair, q))

    def take_last():
        wait(taken, give_recv)
        end_high[128 : 128 + SLC, :], end_low[128 : 128 + SLC, :] = split(taken[...])

    for k in range(STEPS):
        ready = {0: (1, 2, 3), 1: (2, 3), 2: (3,), 3: ()}[k]
        pending = q >= 0
        for c in ready:
            pending = pending & (q != c)

        @pl.when(pending)
        def _():
            load_panel(k).wait()

    cut_last()

    @pl.when((q > 2) & jnp.logical_not(is_chain))
    def _():
        exchange_last()

    @pl.when(is_relay)
    def _():
        hand_on(0)

    lax.fori_loop(0, STEPS - 1, cut_block, 0)

    def add_piece(k):
        if k:
            for n in range(len(CHAIN)):
                pieces[k, PART * n : PART * (n + 1), :] = parts[k - 1, n]
        piece = pieces[k, :, 0:SLC]
        for n in range(0, ROWS, 2):
            at = slice(128 * n, 128 * (n + 2))
            term = dot3(piece, (cut_high[k, :, at], cut_low[k, :, at]), 0)
            for h in range(2):
                value = term[:, 128 * h : 128 * (h + 1)]
                if k == 0:
                    acc[n + h] = value
                else:
                    acc[n + h] += value

    wide = lax.broadcasted_iota(jnp.int32, (RHS // 4, 128), 1)

    def pack(slot, put):
        rest = acc[slot, TAIL:RHS, :]
        for a in range(3):
            at = slice(RHS // 4 * a, RHS // 4 * (a + 1))
            put(at, jnp.where(wide < SLC, acc[slot, at, :], pltpu.roll(rest, SLC - 32 * a, 1)))

    def exchange_sums():
        for n in range(ROWS // 2):

            def put(at, value):
                near_out[n, at, :] = value

            pack(ROWS // 2 + n, put)
        push(near_out, near_in, near_send, near_recv, (pair, q))

    def far_first(i):
        return lax.rem(p + 8 + (1 - 2 * lax.rem(i, 2)) * lax.div(i + 1, 2), ROWS)

    @pl.when(is_chain)
    def _():
        my_cut = pl.ds(pl.multiple_of(CUT * lax.rem(p, 4), 128), CUT)

        def spread_to(k, to):
            if k == STEPS - 1:
                src, dst = last_mine, last_parts.at[g]
            else:
                src, dst = mine.at[k], parts.at[k - 1, g]
            push(src, dst, piece_send.at[k], piece_recv.at[k], (p, to))

        def spread(k):
            def send(i, _):
                spread_to(k, lax.rem(q + i, COLS))
                return 0

            lax.fori_loop(1, COLS, send, 0)

        def others(k):
            wait(parts.at[k - 1, pl.ds(0, len(CHAIN) - 1)], piece_recv.at[k])
            parts[k - 1, g] = mine[k]

        for k in range(1, STEPS):
            load_inverse(k).wait()
            if k < STEPS - 1:
                inv_high[k], inv_low[k] = split(inv[k])
        none = jnp.zeros((128 - SLC, BLK), BF16)
        for ref, value in zip((last_high, last_low), split(inv[STEPS - 1])):
            ref[0:SLC, :] = value
            ref[SLC:128, :] = none
            ref[128 + SLC :, :] = none

        for k in range(1, STEPS):
            wait(base_in.at[k - 1], base_recv.at[k - 1])
            if k == 1:
                rs_out[0] = base_in[0]
            else:
                rs_out[k - 1] = base_in[k - 1] - dot3(mine[k - 1, :, 0:SLC], block(k - 2), 0)

            def scatter(i, _):
                to = far_first(i)
                part = pl.ds(pl.multiple_of(CUT * lax.rem(to, 4), 128), CUT)
                slot = lax.rem(p - to + ROWS, ROWS) - 1
                push(
                    rs_out.at[k - 1, :, part],
                    rs_in.at[k - 1, slot],
                    rs_send.at[k - 1],
                    rs_recv.at[k - 1],
                    (to, q),
                )
                return 0

            lax.fori_loop(0, ROWS - 1, scatter, 0)
            if k == 1:
                exchange_last()
            if k == 1:
                wait(pieces.at[0], piece_recv.at[0])
                add_piece(0)
            else:
                spread(k - 1)
            if k == STEPS - 1:
                wait(inv_other, other_recv)
                last_high[128 : 128 + SLC, :], last_low[128 : 128 + SLC, :] = split(inv_other[...])
                take_last()

            wait(rs_in.at[k - 1], rs_recv.at[k - 1])
            total = rs_out[k - 1, :, my_cut]
            for n in range(ROWS - 1):
                total = total + rs_in[k - 1, n]
            residue[k - 1, :, my_cut] = total
            for d in (2, -1, 1):
                push(
                    residue.at[k - 1, :, my_cut],
                    residue.at[k - 1, :, my_cut],
                    ag_send.at[k - 1],
                    ag_recv.at[k - 1],
                    (lax.rem(p - d + ROWS, ROWS), q),
                )
            if k > 1:
                others(k - 1)
                add_piece(k - 1)
            if k == STEPS - 1:
                exchange_sums()
            if k < STEPS - 1:
                wait_block(k - 1)
                split_block(k - 1, lambda j: rep_flat[k - 1, pl.ds(j, SLC, stride=TILES), :])
            wait(residue.at[k - 1, :, pl.ds(0, 3 * CUT)], ag_recv.at[k - 1])
            if k < STEPS - 1:
                mine[k, :, 0:SLC] = dot3(residue[k - 1], (inv_high[k], inv_low[k]), 1)
                mine[k, :, SLC:] = jnp.zeros((PART, 128 - SLC), F32)
            else:
                both = dot3(residue[k - 1], (last_high[...], last_low[...]), 1)
                last_mine[0] = both[:, :128]
                last_mine[1] = both[:, 128:]

        last = STEPS - 1
        x, y, core = lax.div(q, 8), lax.rem(lax.div(q, 2), 4), lax.rem(q, 2)
        for dx, dy, dc in AROUND:
            to = lax.rem(x + dx, 4) * 8 + lax.rem(y + dy, 4) * 2 + lax.rem(core + dc, 2)
            spread_to(last, to)
        wait(last_parts.at[pl.ds(0, len(CHAIN) - 1)], piece_recv.at[last])
        last_parts[g] = last_mine[...]

    @pl.when(jnp.logical_not(is_chain))
    def _():
        @pl.when(q > 3)
        def _():
            wait(pieces.at[0], piece_recv.at[0])

        add_piece(0)

        @pl.when(is_relay)
        def _():
            hand_on(1)

        wait(parts.at[0], piece_recv.at[1])
        add_piece(1)

        @pl.when(q == 3)
        def _():
            base[...] = base[...] - dot3(pieces[1, :, 0:SLC], block(1), 0)
            send_base(3)

        wait(parts.at[1], piece_recv.at[2])
        add_piece(2)
        exchange_sums()

        @pl.when(q > 2)
        def _():
            take_last()

        @pl.when(q < 3)
        def _():
            none = jnp.zeros((SLC, HALF), BF16)
            end_high[128 : 128 + SLC, :] = none
            end_low[128 : 128 + SLC, :] = none

        wait(last_parts, piece_recv.at[3])

    wait(near_in, near_recv)
    for n in range(len(CHAIN)):
        for h in range(2):
            end_piece[PART * n : PART * (n + 1), 128 * h : 128 * (h + 1)] = last_parts[n, h]
    for n in (6, 4, 2, 0):
        at = slice(128 * n, 128 * (n + 2))
        term = dot3(end_piece[...], (end_high[:, at], end_low[:, at]), 0)
        for slot in (n + 1, n):
            acc[slot] += term[:, 128 * (slot - n) : 128 * (slot - n + 1)]

            def put(at, value):
                packed[slot, at, :] = value + near_in[slot, at, :]

            pack(slot, put)
            if slot:
                push(
                    packed.at[slot],
                    far_in.at[slot - 1],
                    far_send,
                    far_recv,
                    (target(slot), q),
                )

    solved_ref[0 : STEPS - 1] = pieces[:, :, 0:SLC]
    solved_ref[STEPS - 1] = end_piece[:, 0:SLC]

    tile = lax.div(3 * p, 4)
    shift = 32 * lax.rem(3 * p, 4)
    here = right[:, pl.ds(pl.multiple_of(128 * tile, 128), 128)]
    after = right[:, pl.ds(pl.multiple_of(128 * jnp.minimum(tile + 1, TILES - 1), 128), 128)]
    turn = lax.rem(128 - shift, 128)
    lanes = lax.broadcasted_iota(jnp.int32, (RHS, 128), 1)
    total = jnp.where(lanes < 128 - shift, pltpu.roll(here, turn, 1), pltpu.roll(after, turn, 1))

    term = packed[0]
    wait(far_in, far_recv)
    for n in range(ROWS // 2 - 1):
        term = term + far_in[n]
    acc[0] = total
    acc[1, 0:TAIL, :] = term
    updated_ref[0:TAIL, :] = (acc[1, 0:TAIL, :] - acc[0, 0:TAIL, :])[:, 0:SLC]
    last = pltpu.roll(acc[1, RHS // 2 : TAIL, :], SLC, 1)
    last = jnp.where(wide < 64, pltpu.roll(acc[1, RHS // 4 : RHS // 2, :], 64, 1), last)
    last = jnp.where(wide < 32, pltpu.roll(acc[1, 0 : RHS // 4, :], 32, 1), last)
    updated_ref[TAIL:RHS, :] = (last - acc[0, TAIL:RHS, :])[:, 0:SLC]

    wait(near_out, near_send)
    wait(far_in, far_send)

    @pl.when(q > 2)
    def _():
        wait(give, give_send)

    @pl.when(is_beside)
    def _():
        wait(inv_other, other_send)

    @pl.when((q == 0) | (q == 1) | (q == 3))
    def _():
        wait(pieces.at[0], first_send)

    @pl.when((q >= 1) & (q <= 3))
    def _():
        wait(base_out, base_send)

    @pl.when(q == 3)
    def _():
        wait(flat.at[pl.ds(0, (COLS - 4) * RHS)], piece_send.at[0])
        wait(flat.at[pl.ds(0, 9 * THIRD)], rep_send)

    @pl.when(is_relay)
    def _():
        for m in range(2):
            wait(flat, relay_send.at[m])

    @pl.when(is_chain)
    def _():
        for k in range(1, STEPS):
            wait(rs_in.at[k - 1], rs_send.at[k - 1])
            wait(residue.at[k - 1, :, pl.ds(0, 3 * CUT)], ag_send.at[k - 1])
            wait(flat.at[pl.ds(0, (COLS - 1) * PART * (2 if k == STEPS - 1 else 1))], piece_send.at[k])


def body(panel, inverse_blocks, right_side):
    hbm = pl.BlockSpec(memory_space=pltpu.HBM)
    vmem = pl.BlockSpec(memory_space=pltpu.VMEM)
    dma = pltpu.SemaphoreType.DMA
    solved, updated = pl.pallas_call(
        kernel,
        out_shape=(
            pltpu.VMEM((STEPS, RHS, SLC), F32),
            pltpu.VMEM((RHS, SLC), F32),
        ),
        in_specs=[hbm, hbm, hbm],
        out_specs=(vmem, vmem),
        scratch_shapes=[
            pltpu.VMEM((STEPS * SLC * TILES, 128), F32),
            pltpu.VMEM((STEPS - 1, SLC, ROWS * 128), BF16),
            pltpu.VMEM((STEPS - 1, SLC, ROWS * 128), BF16),
            pltpu.VMEM((2, SLC * TILES, 128), F32),
            pltpu.VMEM((2, SLC, BLK), BF16),
            pltpu.VMEM((2, SLC, BLK), BF16),
            pltpu.VMEM((STEPS, SLC, BLK), F32),
            pltpu.VMEM((STEPS, SLC, BLK), BF16),
            pltpu.VMEM((STEPS, SLC, BLK), BF16),
            pltpu.VMEM((RHS * TILES, 128), F32),
            pltpu.VMEM((RHS, BLK), F32),
            pltpu.VMEM((STEPS - 1, RHS, 128), F32),
            pltpu.VMEM((2, len(CHAIN), PART, 128), F32),
            pltpu.VMEM((256, HALF), BF16),
            pltpu.VMEM((256, HALF), BF16),
            pltpu.VMEM((RHS, 256), F32),
            pltpu.VMEM((len(CHAIN), 2, PART, 128), F32),
            pltpu.VMEM((2, PART, 128), F32),
            pltpu.VMEM((SLC, HALF), F32),
            pltpu.VMEM((SLC, HALF), F32),
            pltpu.VMEM((SLC, BLK), F32),
            pltpu.VMEM((256, BLK), BF16),
            pltpu.VMEM((256, BLK), BF16),
            pltpu.VMEM((RHS, BLK), F32),
            pltpu.VMEM((len(CHAIN), PART, BLK), F32),
            pltpu.VMEM((3, PART, BLK), F32),
            pltpu.VMEM((3, PART, BLK), F32),
            pltpu.VMEM((3, ROWS - 1, PART, CUT), F32),
            pltpu.VMEM((3, PART, BLK), F32),
            pltpu.VMEM((STEPS, PART, 128), F32),
            pltpu.VMEM((ROWS, RHS, 128), F32),
            pltpu.VMEM((ROWS // 2, TAIL, 128), F32),
            pltpu.VMEM((ROWS // 2, TAIL, 128), F32),
            pltpu.VMEM((ROWS // 2, TAIL, 128), F32),
            pltpu.VMEM((ROWS // 2 - 1, TAIL, 128), F32),
            dma((STEPS,)),
            dma((STEPS,)),
            dma,
            dma,
            dma((2, 3)),
            pltpu.SemaphoreType.REGULAR,
            dma((2,)),
            dma,
            dma((STEPS,)),
            dma((STEPS,)),
            dma,
            dma((3,)),
            dma((3,)),
            dma((3,)),
            dma((3,)),
            dma((3,)),
            dma,
            dma,
            dma,
            dma,
            dma,
            dma,
            dma,
            dma,
        ],
        compiler_params=pltpu.CompilerParams(collective_id=0, has_side_effects=True, vmem_limit_bytes=61500 * 1024),
        name="solve",
    )(
        panel.reshape(STEPS * SLC * TILES, 128),
        inverse_blocks,
        right_side.reshape(RHS * TILES, 128),
    )
    return jnp.transpose(solved, (1, 0, 2)), -updated.reshape(RHS, 1, 1, SLC)


def solution(mesh):
    placed = (P(None, "row", None, "col", None), P(None, "row", None), P(None, None, "col", None))
    return jax.shard_map(
        body,
        mesh=mesh,
        in_specs=placed,
        out_specs=(P(None, None, "row"), P(None, None, "col", "row")),
        check_vma=False,
    )
```

```python
import jax
import jax.numpy as jnp
from jax import lax
from jax.experimental import pallas as pl
from jax.experimental.pallas import tpu as pltpu
from jax.sharding import PartitionSpec as P

MESH = pl.DeviceIdType.MESH
F32 = jnp.float32
BF16 = jnp.bfloat16
ROWS, COLS = 16, 32
STEPS, RHS, BLK, SLC = 4, 48, 1536, 96
TILES = BLK // 128
CHAIN = (4, 6, 8, 10, 12, 14, 16, 18, 24, 26, 28, 30)
RELAYS = {5: (4, 6, 14, 30), 11: (10, 8, 12, 18), 27: (26, 24, 28, 16)}
THIRD = SLC * BLK // 128 // 3
PART = RHS // len(CHAIN)
CUT = BLK // 4
AROUND = sorted(
    [(x, y, c) for x in range(4) for y in range(4) for c in range(2) if x or y or c],
    key=lambda d: (-min(d[0], 4 - d[0]) - min(d[1], 4 - d[1]), d),
)
TAIL = RHS - RHS // 4
HALF = ROWS // 2 * 128


def hops(first, second):
    total = 0
    for a, b in ((first // 8, second // 8), (first // 2 % 4, second // 2 % 4)):
        total += min(abs(a - b), 4 - abs(a - b))
    return total


def split(value):
    high = value.astype(BF16)
    return high, (value - high.astype(F32)).astype(BF16)


def dot3(left, right, axis):
    rows = left.shape[0]
    high = left.astype(BF16)
    wide = high.astype(F32)
    stacked = jnp.concatenate([wide, left - wide], 0).astype(BF16)
    dims = (((1,), (axis,)), ((), ()))
    both = lax.dot_general(stacked, right[0], dims, preferred_element_type=F32)
    rest = lax.dot_general(high, right[1], dims, preferred_element_type=F32)
    return both[:rows] + (both[rows:] + rest)


def kernel(
    panel_ref,
    inverse_ref,
    right_ref,
    solved_ref,
    updated_ref,
    flat,
    cut_high,
    cut_low,
    rep_flat,
    block_high,
    block_low,
    inv,
    inv_high,
    inv_low,
    right_flat,
    right,
    pieces,
    parts,
    end_high,
    end_low,
    end_piece,
    last_parts,
    last_mine,
    give,
    taken,
    inv_other,
    last_high,
    last_low,
    base,
    base_out,
    base_in,
    rs_out,
    rs_in,
    residue,
    mine,
    acc,
    packed,
    near_out,
    near_in,
    far_in,
    panel_sem,
    inverse_sem,
    right_sem,
    rep_send,
    rep_recv,
    rep_turn,
    relay_send,
    first_send,
    piece_send,
    piece_recv,
    base_send,
    base_recv,
    rs_send,
    rs_recv,
    ag_send,
    ag_recv,
    give_send,
    give_recv,
    other_send,
    other_recv,
    near_send,
    near_recv,
    far_send,
    far_recv,
):
    p = lax.axis_index("row")
    q = lax.axis_index("col")
    is_chain = (lax.rem(q, 2) == 0) & (q > 3) & (q != 20) & (q != 22)
    g = jnp.where(q < 20, lax.div(q - 4, 2), lax.div(q - 8, 2))
    is_relay = (q == 5) | (q == 11) | (q == 27)
    is_beside = (lax.rem(q, 2) == 1) & (q > 3) & (q != 21) & (q != 23)
    side = 2 * lax.rem(p, 2) - 1
    pair = p - side

    def target(slot):
        return lax.rem(p + side * slot + ROWS, ROWS)


    def wait(ref, sem):
        pltpu.make_async_copy(ref, ref, sem).wait()

    def push(src, dst, send, recv, where):
        pltpu.make_async_remote_copy(
            src_ref=src, dst_ref=dst, send_sem=send, recv_sem=recv, device_id=where, device_id_type=MESH
        ).start()

    def load_inverse(k):
        return pltpu.make_async_copy(inverse_ref.at[k], inv.at[k], inverse_sem.at[k])

    def load_panel(k):
        part = pl.ds(k * SLC * TILES, SLC * TILES)
        return pltpu.make_async_copy(panel_ref.at[part], flat.at[part], panel_sem.at[k])

    barrier = pltpu.get_barrier_semaphore()

    def hello(row, col):
        pl.semaphore_signal(barrier, inc=1, device_id=(row, col), device_id_type=MESH)

    @pl.when(is_chain)
    def _():
        def ring(i, _):
            hello(lax.rem(p + 8 + (1 - 2 * lax.rem(i, 2)) * lax.div(i + 1, 2), ROWS), q)
            return 0

        lax.fori_loop(0, ROWS - 1, ring, 0)
        hello(pair, q + 1)

    load_right = pltpu.make_async_copy(right_ref, right_flat, right_sem)
    load_right.start()

    @pl.when(q == 0)
    def _():
        load_inverse(0).start()

    @pl.when(q == 1)
    def _():
        load_panel(0).start()

    @pl.when(q > 1)
    def _():
        for k in range(STEPS):
            load_panel(k).start()

    @pl.when(q == 1)
    def _():
        hello(p, 0)

    @pl.when(is_chain | (q == 3))
    def _():
        hello(p, 1)

    @pl.when((q > 2) & jnp.logical_not(is_chain))
    def _():
        hello(pair, q)

    @pl.when(is_chain | is_relay | (q == 3))
    def _():
        hello(p, 2)

    for r, group in RELAYS.items():

        @pl.when((q == group[0]) | (q == group[1]) | (q == group[2]) | (q == group[3]))
        def _():
            hello(p, r)

    for c in CHAIN:

        @pl.when(q != c)
        def _():
            hello(p, c)

    @pl.when((q == 2) | (q > 3))
    def _():
        hello(p, 3)

    @pl.when(is_chain)
    def _():
        for k in range(1, STEPS):
            load_inverse(k).start()

    load_right.wait()
    for j in range(TILES):
        right[:, 128 * j : 128 * (j + 1)] = right_flat[pl.ds(j, RHS, stride=TILES), :]

    def panel_tile(k, j):
        return flat[pl.ds(k * SLC * TILES + j, SLC, stride=TILES), :]

    def split_block(n, tile):
        for j in range(TILES):
            at = slice(128 * j, 128 * (j + 1))
            block_high[n, :, at], block_low[n, :, at] = split(tile(j))

    own = jnp.where(p == 0, 1.0, 0.0).astype(F32)

    def send_base(k):
        for n, c in sorted(enumerate(CHAIN), key=lambda v: -hops(v[1], k)):
            base_out[n] = base[PART * n : PART * (n + 1), :]
            push(
                base_out.at[n],
                base_in.at[k - 1],
                base_send,
                base_recv.at[k - 1],
                (p, c),
            )

    def block(n):
        return block_high[n], block_low[n]

    @pl.when(q == 0)
    def _():
        load_inverse(0).wait()
        pieces[0, :, 0:SLC] = dot3(right[...], split(inv[0]), 1)
        pl.semaphore_wait(barrier, 1)
        push(pieces.at[0], pieces.at[0], first_send, piece_recv.at[0], (p, 1))
        load_panel(0).start()

    @pl.when(q == 1)
    def _():
        load_panel(0).wait()
        split_block(0, lambda j: panel_tile(0, j))
        pl.semaphore_wait(barrier, len(CHAIN) + 1)
        wait(pieces.at[0], piece_recv.at[0])
        base[...] = own * right[...] - dot3(pieces[0, :, 0:SLC], block(0), 0)
        send_base(1)
        push(pieces.at[0], pieces.at[0], first_send, piece_recv.at[0], (p, 3))

    @pl.when(q < 2)
    def _():
        for k in range(1, STEPS):
            load_panel(k).start()

    def send_block(k):
        for n in range(3):
            for r in RELAYS:
                push(
                    flat.at[pl.ds((k - 1) * SLC * TILES + n * THIRD, THIRD)],
                    rep_flat.at[k - 2, pl.ds(n * THIRD, THIRD)],
                    rep_send,
                    rep_recv.at[k - 2, n],
                    (p, r),
                )

    def hand_on(m):
        for n in range(3):
            part = rep_flat.at[m, pl.ds(n * THIRD, THIRD)]
            wait(part, rep_recv.at[m, n])
            for r, group in RELAYS.items():

                @pl.when(q == r)
                def _():
                    for c in group:
                        push(part, part, relay_send.at[m], rep_recv.at[m, n], (p, c))

    def wait_block(m):
        for n in range(3):
            wait(rep_flat.at[m, pl.ds(n * THIRD, THIRD)], rep_recv.at[m, n])

    @pl.when(q == 2)
    def _():
        load_panel(1).wait()
        pl.semaphore_wait(barrier, len(CHAIN) + len(RELAYS) + 1)
        send_block(2)
        load_panel(0).wait()
        split_block(0, lambda j: panel_tile(0, j))
        wait(pieces.at[0], piece_recv.at[0])
        base[...] = own * right[...] - dot3(pieces[0, :, 0:SLC], block(0), 0)
        send_base(2)
        wait(flat.at[pl.ds(0, 9 * THIRD)], rep_send)
        pl.semaphore_signal(rep_turn, inc=1, device_id=(p, 3), device_id_type=MESH)

    @pl.when(q == 3)
    def _():
        for k in range(2):
            load_panel(k).wait()
            split_block(k, lambda j: panel_tile(k, j))
        load_panel(2).wait()
        pl.semaphore_wait(barrier, COLS - 3 + 1)
        wait(pieces.at[0], piece_recv.at[0])
        push(pieces.at[0], pieces.at[0], first_send, piece_recv.at[0], (p, 2))

        def spread_first(i, _):
            push(pieces.at[0], pieces.at[0], piece_send.at[0], piece_recv.at[0], (p, i))
            return 0

        lax.fori_loop(4, COLS, spread_first, 0)
        base[...] = own * right[...] - dot3(pieces[0, :, 0:SLC], block(0), 0)
        pl.semaphore_wait(rep_turn, 1)
        send_block(3)

    @pl.when(is_chain)
    def _():
        pl.semaphore_wait(barrier, ROWS - 1 + COLS - 1)

    @pl.when((q > 3) & jnp.logical_not(is_chain | is_beside))
    def _():
        pl.semaphore_wait(barrier, 1)

    @pl.when(is_beside & jnp.logical_not(is_relay))
    def _():
        pl.semaphore_wait(barrier, 2)

    @pl.when(is_relay)
    def _():
        pl.semaphore_wait(barrier, 2 + 4)

    @pl.when(is_beside)
    def _():
        push(inverse_ref.at[STEPS - 1], inv_other, other_send, other_recv, (pair, q - 1))

    lane = lax.broadcasted_iota(jnp.int32, (SLC, 128), 1)

    def cut_tile(k, slot):
        n = target(slot) if slot < ROWS // 2 else lax.rem(pair - side * (slot - ROWS // 2) + ROWS, ROWS)
        tile, shift = lax.div(3 * n, 4), 32 * lax.rem(3 * n, 4)
        turn = lax.rem(128 - shift, 128)
        value = pltpu.roll(panel_tile(k, tile), turn, 1)
        after = pltpu.roll(panel_tile(k, jnp.minimum(tile + 1, TILES - 1)), turn, 1)
        return jnp.where(lane < 128 - shift, value, after)

    def cut_block(k, _):
        for n in range(ROWS):
            at = slice(128 * n, 128 * (n + 1))
            cut_high[k, :, at], cut_low[k, :, at] = split(cut_tile(k, n))
        return 0

    def cut_last():
        none = jnp.zeros((128 - SLC, HALF), BF16)
        for ref in (end_high, end_low):
            ref[SLC:128, :] = none
            ref[128 + SLC :, :] = none
        for n in range(ROWS // 2):
            at = slice(128 * n, 128 * (n + 1))
            end_high[0:SLC, at], end_low[0:SLC, at] = split(cut_tile(STEPS - 1, n))
            give[:, at] = cut_tile(STEPS - 1, ROWS // 2 + n)

    def exchange_last():
        push(give, taken, give_send, give_recv, (pair, q))

    def take_last():
        wait(taken, give_recv)
        end_high[128 : 128 + SLC, :], end_low[128 : 128 + SLC, :] = split(taken[...])

    for k in range(STEPS):
        ready = {0: (1, 2, 3), 1: (2, 3), 2: (3,), 3: ()}[k]
        pending = q >= 0
        for c in ready:
            pending = pending & (q != c)

        @pl.when(pending)
        def _():
            load_panel(k).wait()

    cut_last()

    @pl.when((q > 2) & jnp.logical_not(is_chain))
    def _():
        exchange_last()

    @pl.when(is_relay)
    def _():
        hand_on(0)

    lax.fori_loop(0, STEPS - 1, cut_block, 0)

    def add_piece(k):
        if k:
            for n in range(len(CHAIN)):
                pieces[k, PART * n : PART * (n + 1), :] = parts[k - 1, n]
        piece = pieces[k, :, 0:SLC]
        for n in range(0, ROWS, 2):
            at = slice(128 * n, 128 * (n + 2))
            term = dot3(piece, (cut_high[k, :, at], cut_low[k, :, at]), 0)
            for h in range(2):
                value = term[:, 128 * h : 128 * (h + 1)]
                if k == 0:
                    acc[n + h] = value
                else:
                    acc[n + h] += value

    wide = lax.broadcasted_iota(jnp.int32, (RHS // 4, 128), 1)

    def pack(slot, put):
        rest = acc[slot, TAIL:RHS, :]
        for a in range(3):
            at = slice(RHS // 4 * a, RHS // 4 * (a + 1))
            put(at, jnp.where(wide < SLC, acc[slot, at, :], pltpu.roll(rest, SLC - 32 * a, 1)))

    def exchange_sums():
        for n in range(ROWS // 2):

            def put(at, value):
                near_out[n, at, :] = value

            pack(ROWS // 2 + n, put)
        push(near_out, near_in, near_send, near_recv, (pair, q))

    def far_first(i):
        return lax.rem(p + 8 + (1 - 2 * lax.rem(i, 2)) * lax.div(i + 1, 2), ROWS)

    @pl.when(is_chain)
    def _():
        my_cut = pl.ds(pl.multiple_of(CUT * lax.rem(p, 4), 128), CUT)

        def spread_to(k, to):
            if k == STEPS - 1:
                src, dst = last_mine, last_parts.at[g]
            else:
                src, dst = mine.at[k], parts.at[k - 1, g]
            push(src, dst, piece_send.at[k], piece_recv.at[k], (p, to))

        def spread(k):
            def send(i, _):
                spread_to(k, lax.rem(q + i, COLS))
                return 0

            lax.fori_loop(1, COLS, send, 0)

        def others(k):
            wait(parts.at[k - 1, pl.ds(0, len(CHAIN) - 1)], piece_recv.at[k])
            parts[k - 1, g] = mine[k]

        for k in range(1, STEPS):
            load_inverse(k).wait()
            if k < STEPS - 1:
                inv_high[k], inv_low[k] = split(inv[k])
        none = jnp.zeros((128 - SLC, BLK), BF16)
        for ref, value in zip((last_high, last_low), split(inv[STEPS - 1])):
            ref[0:SLC, :] = value
            ref[SLC:128, :] = none
            ref[128 + SLC :, :] = none

        for k in range(1, STEPS):
            wait(base_in.at[k - 1], base_recv.at[k - 1])
            if k == 1:
                rs_out[0] = base_in[0]
            else:
                rs_out[k - 1] = base_in[k - 1] - dot3(mine[k - 1, :, 0:SLC], block(k - 2), 0)

            def scatter(i, _):
                to = far_first(i)
                part = pl.ds(pl.multiple_of(CUT * lax.rem(to, 4), 128), CUT)
                slot = lax.rem(p - to + ROWS, ROWS) - 1
                push(
                    rs_out.at[k - 1, :, part],
                    rs_in.at[k - 1, slot],
                    rs_send.at[k - 1],
                    rs_recv.at[k - 1],
                    (to, q),
                )
                return 0

            lax.fori_loop(0, ROWS - 1, scatter, 0)
            if k == 1:
                exchange_last()
            if k == 1:
                wait(pieces.at[0], piece_recv.at[0])
                add_piece(0)
            else:
                spread(k - 1)
            if k == STEPS - 1:
                wait(inv_other, other_recv)
                last_high[128 : 128 + SLC, :], last_low[128 : 128 + SLC, :] = split(inv_other[...])
                take_last()

            wait(rs_in.at[k - 1], rs_recv.at[k - 1])
            total = rs_out[k - 1, :, my_cut]
            for n in range(ROWS - 1):
                total = total + rs_in[k - 1, n]
            residue[k - 1, :, my_cut] = total
            for d in (2, -1, 1):
                push(
                    residue.at[k - 1, :, my_cut],
                    residue.at[k - 1, :, my_cut],
                    ag_send.at[k - 1],
                    ag_recv.at[k - 1],
                    (lax.rem(p - d + ROWS, ROWS), q),
                )
            if k > 1:
                others(k - 1)
                add_piece(k - 1)
            if k == STEPS - 1:
                exchange_sums()
            if k < STEPS - 1:
                wait_block(k - 1)
                split_block(k - 1, lambda j: rep_flat[k - 1, pl.ds(j, SLC, stride=TILES), :])
            wait(residue.at[k - 1, :, pl.ds(0, 3 * CUT)], ag_recv.at[k - 1])
            if k < STEPS - 1:
                mine[k, :, 0:SLC] = dot3(residue[k - 1], (inv_high[k], inv_low[k]), 1)
                mine[k, :, SLC:] = jnp.zeros((PART, 128 - SLC), F32)
            else:
                both = dot3(residue[k - 1], (last_high[...], last_low[...]), 1)
                last_mine[0] = both[:, :128]
                last_mine[1] = both[:, 128:]

        last = STEPS - 1
        x, y, core = lax.div(q, 8), lax.rem(lax.div(q, 2), 4), lax.rem(q, 2)
        for dx, dy, dc in AROUND:
            to = lax.rem(x + dx, 4) * 8 + lax.rem(y + dy, 4) * 2 + lax.rem(core + dc, 2)
            spread_to(last, to)
        wait(last_parts.at[pl.ds(0, len(CHAIN) - 1)], piece_recv.at[last])
        last_parts[g] = last_mine[...]

    @pl.when(jnp.logical_not(is_chain))
    def _():
        @pl.when(q > 3)
        def _():
            wait(pieces.at[0], piece_recv.at[0])

        add_piece(0)

        @pl.when(is_relay)
        def _():
            hand_on(1)

        wait(parts.at[0], piece_recv.at[1])
        add_piece(1)

        @pl.when(q == 3)
        def _():
            base[...] = base[...] - dot3(pieces[1, :, 0:SLC], block(1), 0)
            send_base(3)

        wait(parts.at[1], piece_recv.at[2])
        add_piece(2)
        exchange_sums()

        @pl.when(q > 2)
        def _():
            take_last()

        @pl.when(q < 3)
        def _():
            none = jnp.zeros((SLC, HALF), BF16)
            end_high[128 : 128 + SLC, :] = none
            end_low[128 : 128 + SLC, :] = none

        wait(last_parts, piece_recv.at[3])

    wait(near_in, near_recv)
    for n in range(len(CHAIN)):
        for h in range(2):
            end_piece[PART * n : PART * (n + 1), 128 * h : 128 * (h + 1)] = last_parts[n, h]
    for n in (6, 4, 2, 0):
        at = slice(128 * n, 128 * (n + 2))
        term = dot3(end_piece[...], (end_high[:, at], end_low[:, at]), 0)
        for slot in (n + 1, n):
            acc[slot] += term[:, 128 * (slot - n) : 128 * (slot - n + 1)]

            def put(at, value):
                packed[slot, at, :] = value + near_in[slot, at, :]

            pack(slot, put)
            if slot:
                push(
                    packed.at[slot],
                    far_in.at[slot - 1],
                    far_send,
                    far_recv,
                    (target(slot), q),
                )

    solved_ref[0 : STEPS - 1] = pieces[:, :, 0:SLC]
    solved_ref[STEPS - 1] = end_piece[:, 0:SLC]

    tile = lax.div(3 * p, 4)
    shift = 32 * lax.rem(3 * p, 4)
    here = right[:, pl.ds(pl.multiple_of(128 * tile, 128), 128)]
    after = right[:, pl.ds(pl.multiple_of(128 * jnp.minimum(tile + 1, TILES - 1), 128), 128)]
    turn = lax.rem(128 - shift, 128)
    lanes = lax.broadcasted_iota(jnp.int32, (RHS, 128), 1)
    total = jnp.where(lanes < 128 - shift, pltpu.roll(here, turn, 1), pltpu.roll(after, turn, 1))

    term = packed[0]
    wait(far_in, far_recv)
    for n in range(ROWS // 2 - 1):
        term = term + far_in[n]
    acc[0] = total
    acc[1, 0:TAIL, :] = term
    updated_ref[0:TAIL, :] = (acc[1, 0:TAIL, :] - acc[0, 0:TAIL, :])[:, 0:SLC]
    last = pltpu.roll(acc[1, RHS // 2 : TAIL, :], SLC, 1)
    last = jnp.where(wide < 64, pltpu.roll(acc[1, RHS // 4 : RHS // 2, :], 64, 1), last)
    last = jnp.where(wide < 32, pltpu.roll(acc[1, 0 : RHS // 4, :], 32, 1), last)
    updated_ref[TAIL:RHS, :] = (last - acc[0, TAIL:RHS, :])[:, 0:SLC]

    wait(near_out, near_send)
    wait(far_in, far_send)

    @pl.when(q > 2)
    def _():
        wait(give, give_send)

    @pl.when(is_beside)
    def _():
        wait(inv_other, other_send)

    @pl.when((q == 0) | (q == 1) | (q == 3))
    def _():
        wait(pieces.at[0], first_send)

    @pl.when((q >= 1) & (q <= 3))
    def _():
        wait(base_out, base_send)

    @pl.when(q == 3)
    def _():
        wait(flat.at[pl.ds(0, (COLS - 4) * RHS)], piece_send.at[0])
        wait(flat.at[pl.ds(0, 9 * THIRD)], rep_send)

    @pl.when(is_relay)
    def _():
        for m in range(2):
            wait(flat, relay_send.at[m])

    @pl.when(is_chain)
    def _():
        for k in range(1, STEPS):
            wait(rs_in.at[k - 1], rs_send.at[k - 1])
            wait(residue.at[k - 1, :, pl.ds(0, 3 * CUT)], ag_send.at[k - 1])
            wait(flat.at[pl.ds(0, (COLS - 1) * PART * (2 if k == STEPS - 1 else 1))], piece_send.at[k])


def body(panel, inverse_blocks, right_side):
    hbm = pl.BlockSpec(memory_space=pltpu.HBM)
    vmem = pl.BlockSpec(memory_space=pltpu.VMEM)
    dma = pltpu.SemaphoreType.DMA
    solved, updated = pl.pallas_call(
        kernel,
        out_shape=(
            pltpu.VMEM((STEPS, RHS, SLC), F32),
            pltpu.VMEM((RHS, SLC), F32),
        ),
        in_specs=[hbm, hbm, hbm],
        out_specs=(vmem, vmem),
        scratch_shapes=[
            pltpu.VMEM((STEPS * SLC * TILES, 128), F32),
            pltpu.VMEM((STEPS - 1, SLC, ROWS * 128), BF16),
            pltpu.VMEM((STEPS - 1, SLC, ROWS * 128), BF16),
            pltpu.VMEM((2, SLC * TILES, 128), F32),
            pltpu.VMEM((2, SLC, BLK), BF16),
            pltpu.VMEM((2, SLC, BLK), BF16),
            pltpu.VMEM((STEPS, SLC, BLK), F32),
            pltpu.VMEM((STEPS, SLC, BLK), BF16),
            pltpu.VMEM((STEPS, SLC, BLK), BF16),
            pltpu.VMEM((RHS * TILES, 128), F32),
            pltpu.VMEM((RHS, BLK), F32),
            pltpu.VMEM((STEPS - 1, RHS, 128), F32),
            pltpu.VMEM((2, len(CHAIN), PART, 128), F32),
            pltpu.VMEM((256, HALF), BF16),
            pltpu.VMEM((256, HALF), BF16),
            pltpu.VMEM((RHS, 256), F32),
            pltpu.VMEM((len(CHAIN), 2, PART, 128), F32),
            pltpu.VMEM((2, PART, 128), F32),
            pltpu.VMEM((SLC, HALF), F32),
            pltpu.VMEM((SLC, HALF), F32),
            pltpu.VMEM((SLC, BLK), F32),
            pltpu.VMEM((256, BLK), BF16),
            pltpu.VMEM((256, BLK), BF16),
            pltpu.VMEM((RHS, BLK), F32),
            pltpu.VMEM((len(CHAIN), PART, BLK), F32),
            pltpu.VMEM((3, PART, BLK), F32),
            pltpu.VMEM((3, PART, BLK), F32),
            pltpu.VMEM((3, ROWS - 1, PART, CUT), F32),
            pltpu.VMEM((3, PART, BLK), F32),
            pltpu.VMEM((STEPS, PART, 128), F32),
            pltpu.VMEM((ROWS, RHS, 128), F32),
            pltpu.VMEM((ROWS // 2, TAIL, 128), F32),
            pltpu.VMEM((ROWS // 2, TAIL, 128), F32),
            pltpu.VMEM((ROWS // 2, TAIL, 128), F32),
            pltpu.VMEM((ROWS // 2 - 1, TAIL, 128), F32),
            dma((STEPS,)),
            dma((STEPS,)),
            dma,
            dma,
            dma((2, 3)),
            pltpu.SemaphoreType.REGULAR,
            dma((2,)),
            dma,
            dma((STEPS,)),
            dma((STEPS,)),
            dma,
            dma((3,)),
            dma((3,)),
            dma((3,)),
            dma((3,)),
            dma((3,)),
            dma,
            dma,
            dma,
            dma,
            dma,
            dma,
            dma,
            dma,
        ],
        compiler_params=pltpu.CompilerParams(collective_id=0, has_side_effects=True, vmem_limit_bytes=61500 * 1024),
        name="solve",
    )(
        panel.reshape(STEPS * SLC * TILES, 128),
        inverse_blocks,
        right_side.reshape(RHS * TILES, 128),
    )
    return jnp.transpose(solved, (1, 0, 2)), -updated.reshape(RHS, 1, 1, SLC)


def solution(mesh):
    placed = (P(None, "row", None, "col", None), P(None, "row", None), P(None, None, "col", None))
    return jax.shard_map(
        body,
        mesh=mesh,
        in_specs=placed,
        out_specs=(P(None, None, "row"), P(None, None, "col", "row")),
        check_vma=False,
    )
```
